128 devices in a mesh: row: 8 (over x, core), col: 16 (over y, z).
Axes of the slice: x: 4, y: 4, z: 4, core: 2. Of those that a mesh axis runs over, the one named last changes fastest.
Arguments:
- trail: bfloat16 [16384, 16384], P('row', 'col'), may hold values from -0.046875 to 0.046875
- row_one: bfloat16 [128, 16384], P('row', 'col'), may hold values from -0.5 to 0.5
- row_two: bfloat16 [128, 16384], P('row', 'col'), may hold values from -0.5 to 0.5
- diag_one: float32 [128, 128], replicated, may hold values from -1 to 2, as said below
- diag_two: float32 [128, 128], replicated, may hold values from -1 to 2, as said below
- adj_trail: float32 [16384, 16384], P('row', 'col'), may hold values from -6 to 6
- adj_row_one: float32 [128, 16384], P('row', 'col'), may hold values from -6 to 6
- adj_row_two: float32 [128, 16384], P('row', 'col'), may hold values from -6 to 6
- adj_diag_one: float32 [128, 128], replicated, may hold values from -6 to 6
- adj_diag_two: float32 [128, 128], replicated, may hold values from -6 to 6
Outputs:
- grad_trail: bfloat16 [16384, 16384], P('row', 'col')
- grad_row_one: float32 [128, 16384], P('row', 'col')
- grad_row_two: float32 [128, 16384], P('row', 'col')
- grad_diag_one: float32 [128, 128], replicated
- grad_diag_two: float32 [128, 128], replicated
The draws below stay inside these ranges and needn't reach their ends.
Inputs may be any that keep to these rules, and one draw needn't show every extreme that they name: `diag_one`: lower triangular with a positive diagonal. `diag_two`: lower triangular with a positive diagonal.
All inputs are finite; a program needn't handle non-finite values.
Results may differ from the reference program's by a relative error of at most 0.014.
Values may be sent and summed in bfloat16 or wider, within the bound.
A program may use at most 128 MiB of HBM per device.

```python
import jax
import jax.numpy as jnp
from jax import lax

PANEL = 128
WC = 1024
M = 16384
W = 16384
N_COL = 16


def lower_block(key, order):
    first, second = jax.random.split(key)
    diagonal = jax.random.uniform(first, (order,), jnp.float32, 1.0, 2.0)
    below = 0.03 * jax.random.normal(second, (order, order), jnp.float32)
    below = jnp.clip(below, -0.5, 0.5)
    return jnp.tril(below, -1) + jnp.diag(diagonal)


def draw_diag_one(key, part):
    return lower_block(jax.random.fold_in(key, 11), PANEL)


def draw_diag_two(key, part):
    return lower_block(jax.random.fold_in(key, 12), PANEL)


def block_scale(own_key, dims, cuts, low, high):
    level = 1.0
    for position, shards_of in cuts:
        heights = jax.random.uniform(jax.random.fold_in(jax.random.fold_in(own_key, 6), position), (shards_of,), jnp.float32, low / len(cuts), high / len(cuts))
        level = level * jnp.repeat(jnp.exp(heights), dims[position] // shards_of).reshape((-1,) + (1,) * (len(dims) - 1 - position))
    return level


def scatter_about(rng, extent, spread, most, shards=(), kind=jnp.bfloat16):
    loudness = block_scale(rng, extent, shards, -0.22, 0.18) if shards else 1.0
    array = jax.random.normal(rng, extent, jnp.float32) * spread * loudness
    return jnp.minimum(jnp.maximum(array, -most), most).astype(kind)


def setup_inputs(seed: int = 0) -> dict:
    arg_keys = jax.random.split(jax.random.key(seed), 11)
    return {
        "trail": scatter_about(arg_keys[0], (M, W), M ** -0.5, 0.046875, ((0, 8), (1, 16))),
        "row_one": scatter_about(arg_keys[1], (PANEL, W), PANEL ** -0.5, 0.5, ((0, 8), (1, 16))),
        "row_two": scatter_about(arg_keys[2], (PANEL, W), PANEL ** -0.5, 0.5, ((0, 8), (1, 16))),
        "diag_one": draw_diag_one(jax.random.fold_in(arg_keys[10], 71), 0),
        "diag_two": draw_diag_two(jax.random.fold_in(arg_keys[10], 71), 0),
        "adj_trail": scatter_about(arg_keys[5], (M, W), 1.0, 6.0, ((0, 8), (1, 16)), jnp.float32),
        "adj_row_one": scatter_about(arg_keys[6], (PANEL, W), 1.0, 6.0, ((0, 8), (1, 16)), jnp.float32),
        "adj_row_two": scatter_about(arg_keys[7], (PANEL, W), 1.0, 6.0, ((0, 8), (1, 16)), jnp.float32),
        "adj_diag_one": scatter_about(arg_keys[8], (PANEL, PANEL), 1.0, 6.0, (), jnp.float32),
        "adj_diag_two": scatter_about(arg_keys[9], (PANEL, PANEL), 1.0, 6.0, (), jnp.float32),
    }


exact_mode = lax.Precision.HIGHEST

def halved_lower(matrix):
    order = matrix.shape[0]
    keep = jnp.tril(jnp.ones((order, order), matrix.dtype)) - 0.5 * jnp.eye(order, dtype=matrix.dtype)
    return matrix * keep

def inverse_lower(block):
    ident = jnp.eye(block.shape[0], dtype=block.dtype)
    return lax.linalg.triangular_solve(block, ident, left_side=True, lower=True)

def block_adjoint(block, inverse, seed_adj):
    inner = halved_lower(jnp.dot(block.T, seed_adj, precision=exact_mode))
    middle = jnp.dot(inverse.T, inner, precision=exact_mode)
    return halved_lower(jnp.dot(middle, inverse, precision=exact_mode))

def reference(trail, row_one, row_two, diag_one, diag_two, adj_trail, adj_row_one, adj_row_two, adj_diag_one, adj_diag_two):
    one_start = (N_COL - 1) * WC - PANEL
    two_start = N_COL * WC - PANEL
    one_end = one_start + PANEL
    inverse_two = inverse_lower(diag_two)
    solved_two = jnp.dot(adj_trail[:, two_start:], inverse_two, precision=exact_mode).astype(jnp.bfloat16)
    seed_two = jnp.tril(adj_diag_two - jnp.dot(solved_two.T.astype(jnp.float32), trail[:, two_start:].astype(jnp.float32), preferred_element_type=jnp.float32))
    grad_diag_two = block_adjoint(diag_two, inverse_two, seed_two)
    mirror_two = grad_diag_two + grad_diag_two.T
    adj_two = adj_row_two - jnp.dot(solved_two.T.astype(jnp.float32), trail.astype(jnp.float32), preferred_element_type=jnp.float32) - jnp.dot(mirror_two, row_two.astype(jnp.float32), precision=exact_mode)
    adj_next = adj_trail - jnp.dot(solved_two.astype(jnp.float32), row_two.astype(jnp.float32), preferred_element_type=jnp.float32)
    inverse_one = inverse_lower(diag_one)
    stacked = jnp.concatenate([adj_two[:, one_start:one_end], adj_next[:, one_start:one_end]], 0)
    solved_one = jnp.dot(stacked, inverse_one, precision=exact_mode).astype(jnp.bfloat16)
    head_rows = solved_one[:PANEL]
    tail_rows = solved_one[PANEL:]
    cross_one = jnp.dot(head_rows.T.astype(jnp.float32), row_two[:, one_start:one_end].astype(jnp.float32), preferred_element_type=jnp.float32) + jnp.dot(tail_rows.T.astype(jnp.float32), trail[:, one_start:one_end].astype(jnp.float32), preferred_element_type=jnp.float32)
    seed_one = jnp.tril(adj_diag_one - cross_one)
    grad_diag_one = block_adjoint(diag_one, inverse_one, seed_one)
    mirror_one = grad_diag_one + grad_diag_one.T
    two_left = adj_two - jnp.dot(head_rows.astype(jnp.float32), row_one.astype(jnp.float32), preferred_element_type=jnp.float32)
    trail_left = adj_next - jnp.dot(tail_rows.astype(jnp.float32), row_one.astype(jnp.float32), preferred_element_type=jnp.float32)
    one_left = adj_row_one - jnp.dot(head_rows.T.astype(jnp.float32), row_two.astype(jnp.float32), preferred_element_type=jnp.float32) - jnp.dot(tail_rows.T.astype(jnp.float32), trail.astype(jnp.float32), preferred_element_type=jnp.float32) - jnp.dot(mirror_one, row_one.astype(jnp.float32), precision=exact_mode)
    grad_trail = trail_left.at[:, one_start:one_end].set(tail_rows.astype(jnp.float32))
    grad_trail = grad_trail.at[:, two_start:].set(solved_two.astype(jnp.float32)).astype(jnp.bfloat16)
    grad_row_one = one_left.at[:, one_start:one_end].set(0.0).at[:, two_start:].set(0.0)
    grad_row_two = two_left.at[:, one_start:one_end].set(head_rows.astype(jnp.float32)).at[:, two_start:].set(0.0)
    return (grad_trail, grad_row_one, grad_row_two, grad_diag_one, grad_diag_two)
```

```python
import jax
import jax.numpy as jnp
from jax import lax
from jax.sharding import PartitionSpec as P

exact_mode = lax.Precision.HIGHEST


def tree_broadcast(value, axis, size, root):
    here = lax.axis_index(axis) ^ root
    step = 1
    while step < size:
        pairs = [(root ^ d, root ^ (d + step)) for d in range(step)]
        arrived = lax.ppermute(value, axis, pairs)
        take = (here >= step) & (here < 2 * step)
        value = jnp.where(take, arrived, value)
        step *= 2
    return value


def butterfly_sum(value, axis, size):
    step = 1
    while step < size:
        pairs = [(i, i ^ step) for i in range(size)]
        value = value + lax.ppermute(value, axis, pairs)
        step *= 2
    return value


def halving_scatter(value, axis, size):
    here = lax.axis_index(axis)
    band = value.shape[0] // size
    blocks = value.reshape(size, band, value.shape[1])
    step = size // 2
    while step >= 1:
        halves = blocks.reshape(2, step, band, value.shape[1])
        high = ((here // step) % 2) == 1
        keep = jnp.where(high, halves[1], halves[0])
        send = jnp.where(high, halves[0], halves[1])
        pairs = [(i, i ^ step) for i in range(size)]
        blocks = keep + lax.ppermute(send, axis, pairs)
        step //= 2
    return blocks.reshape(band, value.shape[1])


def doubling_gather(value, axis, size):
    here = lax.axis_index(axis)
    step = 1
    while step < size:
        pairs = [(i, i ^ step) for i in range(size)]
        other = lax.ppermute(value, axis, pairs)
        high = ((here // step) % 2) == 1
        value = jnp.where(
            high,
            jnp.concatenate([other, value], 0),
            jnp.concatenate([value, other], 0),
        )
        step *= 2
    return value


def halved_lower(matrix):
    order = matrix.shape[0]
    keep = jnp.tril(jnp.ones((order, order), matrix.dtype)) - 0.5 * jnp.eye(
        order, dtype=matrix.dtype
    )
    return matrix * keep


def inverse_lower(block):
    ident = jnp.eye(block.shape[0], dtype=block.dtype)
    return lax.linalg.triangular_solve(block, ident, left_side=True, lower=True)


def block_adjoint(block, inverse, seed_adj):
    inner = halved_lower(jnp.dot(block.T, seed_adj, precision=exact_mode))
    middle = jnp.dot(inverse.T, inner, precision=exact_mode)
    return halved_lower(jnp.dot(middle, inverse, precision=exact_mode))


def make_per_device(n_row, n_col):
    def per_device(
        trail,
        row_one,
        row_two,
        diag_one,
        diag_two,
        adj_trail,
        adj_row_one,
        adj_row_two,
        adj_diag_one,
        adj_diag_two,
    ):
        panel = diag_one.shape[0]
        width = trail.shape[1]
        band = row_one.shape[0]
        last = width - panel
        col_here = lax.axis_index("col")
        row_start = lax.axis_index("row") * band
        root_one = n_col - 2
        root_two = n_col - 1
        here_one = col_here == root_one
        here_two = col_here == root_two
        full_one = doubling_gather(row_one, "row", n_row)
        full_two = doubling_gather(row_two, "row", n_row)

        def own_rows(matrix):
            return lax.dynamic_slice_in_dim(matrix, row_start, band, 0)

        def solve_panel(rows, inverse, root):
            local = jnp.dot(rows, inverse, precision=exact_mode).astype(jnp.bfloat16)
            return tree_broadcast(local, "col", n_col, root)

        def summed_block(partial_value, root):
            rows_sum = butterfly_sum(partial_value, "row", n_row)
            return tree_broadcast(rows_sum, "col", n_col, root)

        inverse_two = inverse_lower(diag_two)
        solved_two = solve_panel(adj_trail[:, last:], inverse_two, root_two)
        partial_two = jnp.dot(solved_two.T, trail[:, last:], preferred_element_type=jnp.float32)
        seed_two = jnp.tril(adj_diag_two - summed_block(partial_two, root_two))
        grad_diag_two = block_adjoint(diag_two, inverse_two, seed_two)
        mirror_two = own_rows(grad_diag_two + grad_diag_two.T)
        rest_two = jnp.dot(mirror_two, full_two.astype(jnp.float32), precision=exact_mode)
        inverse_one = inverse_lower(diag_one)
        crossed = halving_scatter(
            jnp.dot(solved_two.T, trail, preferred_element_type=jnp.float32), "row", n_row
        )
        adj_two = adj_row_two - crossed - rest_two
        adj_next = adj_trail - jnp.dot(solved_two, full_two, preferred_element_type=jnp.float32)
        stacked = jnp.concatenate([adj_two[:, last:], adj_next[:, last:]], 0)
        solved_one = solve_panel(stacked, inverse_one, root_one)
        head_rows = solved_one[:band]
        tail_rows = solved_one[band:]
        partial_one = jnp.dot(
            head_rows.T, row_two[:, last:], preferred_element_type=jnp.float32
        ) + jnp.dot(tail_rows.T, trail[:, last:], preferred_element_type=jnp.float32)
        seed_one = jnp.tril(adj_diag_one - summed_block(partial_one, root_one))
        grad_diag_one = block_adjoint(diag_one, inverse_one, seed_one)
        mirror_one = own_rows(grad_diag_one + grad_diag_one.T)
        rest_one = jnp.dot(mirror_one, full_one.astype(jnp.float32), precision=exact_mode)
        head_update = jnp.dot(head_rows, full_one, preferred_element_type=jnp.float32)
        two_left = adj_two - head_update
        trail_left = adj_next - jnp.dot(tail_rows, full_one, preferred_element_type=jnp.float32)
        crossed_one = halving_scatter(
            jnp.dot(head_rows.T, row_two, preferred_element_type=jnp.float32)
            + jnp.dot(tail_rows.T, trail, preferred_element_type=jnp.float32),
            "row",
            n_row,
        )
        one_left = adj_row_one - crossed_one - rest_one
        trail_block = jnp.where(
            here_one,
            tail_rows.astype(jnp.float32),
            jnp.where(here_two, solved_two.astype(jnp.float32), trail_left[:, last:]),
        )
        grad_trail = jnp.concatenate([trail_left[:, :last], trail_block], 1).astype(jnp.bfloat16)
        zero_block = jnp.zeros((band, panel), jnp.float32)
        one_block = jnp.where(here_one | here_two, zero_block, one_left[:, last:])
        grad_row_one = jnp.concatenate([one_left[:, :last], one_block], 1)
        two_block = jnp.where(
            here_one, head_rows.astype(jnp.float32), jnp.where(here_two, zero_block, two_left[:, last:])
        )
        grad_row_two = jnp.concatenate([two_left[:, :last], two_block], 1)
        return (grad_trail, grad_row_one, grad_row_two, grad_diag_one, grad_diag_two)

    return per_device


def solution(mesh):
    in_specs = (
        P("row", "col"),
        P("row", "col"),
        P("row", "col"),
        P(),
        P(),
        P("row", "col"),
        P("row", "col"),
        P("row", "col"),
        P(),
        P(),
    )
    out_specs = (P("row", "col"), P("row", "col"), P("row", "col"), P(), P())
    return jax.shard_map(
        make_per_device(mesh.shape["row"], mesh.shape["col"]),
        mesh=mesh,
        in_specs=in_specs,
        out_specs=out_specs,
        check_vma=False,
    )
```

```python
import jax
import jax.numpy as jnp
from jax import lax
from jax.sharding import PartitionSpec as P

exact_mode = lax.Precision.HIGHEST


def tree_broadcast(value, axis, size, root):
    here = lax.axis_index(axis) ^ root
    step = 1
    while step < size:
        pairs = [(root ^ d, root ^ (d + step)) for d in range(step)]
        arrived = lax.ppermute(value, axis, pairs)
        take = (here >= step) & (here < 2 * step)
        value = jnp.where(take, arrived, value)
        step *= 2
    return value


def chunked_broadcast(value, axis, size, root, chunks):
    parts = jnp.split(value, chunks, 0)
    return jnp.concatenate([tree_broadcast(p, axis, size, root) for p in parts], 0)


def butterfly_sum(value, axis, size):
    step = 1
    while step < size:
        pairs = [(i, i ^ step) for i in range(size)]
        value = value + lax.ppermute(value, axis, pairs)
        step *= 2
    return value


def halving_scatter(value, axis, size):
    here = lax.axis_index(axis)
    band = value.shape[0] // size
    blocks = value.reshape(size, band, value.shape[1])
    step = size // 2
    while step >= 1:
        halves = blocks.reshape(2, step, band, value.shape[1])
        high = ((here // step) % 2) == 1
        keep = jnp.where(high, halves[1], halves[0])
        send = jnp.where(high, halves[0], halves[1])
        pairs = [(i, i ^ step) for i in range(size)]
        blocks = keep + lax.ppermute(send, axis, pairs)
        step //= 2
    return blocks.reshape(band, value.shape[1])


def doubling_gather(value, axis, size):
    here = lax.axis_index(axis)
    step = 1
    while step < size:
        pairs = [(i, i ^ step) for i in range(size)]
        other = lax.ppermute(value, axis, pairs)
        high = ((here // step) % 2) == 1
        value = jnp.where(
            high,
            jnp.concatenate([other, value], 0),
            jnp.concatenate([value, other], 0),
        )
        step *= 2
    return value


def halved_lower(matrix):
    order = matrix.shape[0]
    keep = jnp.tril(jnp.ones((order, order), matrix.dtype)) - 0.5 * jnp.eye(
        order, dtype=matrix.dtype
    )
    return matrix * keep


def inverse_lower(block):
    ident = jnp.eye(block.shape[0], dtype=block.dtype)
    return lax.linalg.triangular_solve(block, ident, left_side=True, lower=True)


def block_adjoint(block, inverse, seed_adj):
    inner = halved_lower(jnp.dot(block.T, seed_adj, precision=exact_mode))
    middle = jnp.dot(inverse.T, inner, precision=exact_mode)
    return halved_lower(jnp.dot(middle, inverse, precision=exact_mode))


def make_per_device(n_row, n_col):
    def per_device(
        trail,
        row_one,
        row_two,
        diag_one,
        diag_two,
        adj_trail,
        adj_row_one,
        adj_row_two,
        adj_diag_one,
        adj_diag_two,
    ):
        panel = diag_one.shape[0]
        width = trail.shape[1]
        band = row_one.shape[0]
        last = width - panel
        col_here = lax.axis_index("col")
        row_start = lax.axis_index("row") * band
        root_one = n_col - 2
        root_two = n_col - 1
        here_one = col_here == root_one
        here_two = col_here == root_two
        full_one = doubling_gather(row_one, "row", n_row)
        full_two = doubling_gather(row_two, "row", n_row)

        def own_rows(matrix):
            return lax.dynamic_slice_in_dim(matrix, row_start, band, 0)

        def solve_panel(rows, inverse, root):
            local = jnp.dot(rows, inverse, precision=exact_mode).astype(jnp.bfloat16)
            return chunked_broadcast(local, "col", n_col, root, 4)

        def summed_block(partial_value, root):
            rows_sum = butterfly_sum(partial_value, "row", n_row)
            return tree_broadcast(rows_sum, "col", n_col, root)

        inverse_two = inverse_lower(diag_two)
        inverse_one = inverse_lower(diag_one)
        solved_two = solve_panel(adj_trail[:, last:], inverse_two, root_two)
        next_panel = adj_trail[:, last:] - jnp.dot(
            solved_two, full_two[:, last:], preferred_element_type=jnp.float32
        )
        tail_rows = solve_panel(next_panel, inverse_one, root_one)
        partial_two = jnp.dot(solved_two.T, trail[:, last:], preferred_element_type=jnp.float32)
        seed_two = jnp.tril(adj_diag_two - summed_block(partial_two, root_two))
        grad_diag_two = block_adjoint(diag_two, inverse_two, seed_two)
        mirror_two = own_rows(grad_diag_two + grad_diag_two.T)
        rest_two = jnp.dot(mirror_two, full_two.astype(jnp.float32), precision=exact_mode)
        crossed = halving_scatter(
            jnp.dot(solved_two.T, trail, preferred_element_type=jnp.float32), "row", n_row
        )
        adj_two = adj_row_two - crossed - rest_two
        adj_next = adj_trail - jnp.dot(solved_two, full_two, preferred_element_type=jnp.float32)
        head_local = jnp.dot(adj_two[:, last:], inverse_one, precision=exact_mode).astype(
            jnp.bfloat16
        )
        head_rows = tree_broadcast(head_local, "col", n_col, root_one)
        tail_sum = butterfly_sum(
            jnp.dot(tail_rows.T, trail[:, last:], preferred_element_type=jnp.float32), "row", n_row
        )
        head_sum = butterfly_sum(
            jnp.dot(head_local.T, row_two[:, last:], preferred_element_type=jnp.float32), "row", n_row
        )
        seed_one = jnp.tril(
            adj_diag_one - tree_broadcast(head_sum + tail_sum, "col", n_col, root_one)
        )
        grad_diag_one = block_adjoint(diag_one, inverse_one, seed_one)
        mirror_one = own_rows(grad_diag_one + grad_diag_one.T)
        rest_one = jnp.dot(mirror_one, full_one.astype(jnp.float32), precision=exact_mode)
        head_update = jnp.dot(head_rows, full_one, preferred_element_type=jnp.float32)
        two_left = adj_two - head_update
        trail_left = adj_next - jnp.dot(tail_rows, full_one, preferred_element_type=jnp.float32)
        crossed_one = halving_scatter(
            jnp.dot(head_rows.T, row_two, preferred_element_type=jnp.float32)
            + jnp.dot(tail_rows.T, trail, preferred_element_type=jnp.float32),
            "row",
            n_row,
        )
        one_left = adj_row_one - crossed_one - rest_one
        trail_block = jnp.where(
            here_one,
            tail_rows.astype(jnp.float32),
            jnp.where(here_two, solved_two.astype(jnp.float32), trail_left[:, last:]),
        )
        grad_trail = jnp.concatenate([trail_left[:, :last], trail_block], 1).astype(jnp.bfloat16)
        zero_block = jnp.zeros((band, panel), jnp.float32)
        one_block = jnp.where(here_one | here_two, zero_block, one_left[:, last:])
        grad_row_one = jnp.concatenate([one_left[:, :last], one_block], 1)
        two_block = jnp.where(
            here_one, head_rows.astype(jnp.float32), jnp.where(here_two, zero_block, two_left[:, last:])
        )
        grad_row_two = jnp.concatenate([two_left[:, :last], two_block], 1)
        return (grad_trail, grad_row_one, grad_row_two, grad_diag_one, grad_diag_two)

    return per_device


def solution(mesh):
    in_specs = (
        P("row", "col"),
        P("row", "col"),
        P("row", "col"),
        P(),
        P(),
        P("row", "col"),
        P("row", "col"),
        P("row", "col"),
        P(),
        P(),
    )
    out_specs = (P("row", "col"), P("row", "col"), P("row", "col"), P(), P())
    return jax.shard_map(
        make_per_device(mesh.shape["row"], mesh.shape["col"]),
        mesh=mesh,
        in_specs=in_specs,
        out_specs=out_specs,
        check_vma=False,
    )
```

```python
import functools

import jax
import jax.numpy as jnp
from jax import lax
from jax.experimental import pallas as pl
from jax.experimental.pallas import tpu as pltpu
from jax.sharding import PartitionSpec as P

exact_mode = lax.Precision.HIGHEST


def broadcast_kernel(root, size, chunks, x_ref, y_ref, buf, recv_sem, send_sem):
    bits = size.bit_length() - 1
    me = lax.axis_index("col")
    row = lax.axis_index("row")
    rel_bits = []
    for j in range(bits):
        b = (me // (1 << j)) % 2
        rel_bits.append(1 - b if (root >> j) & 1 else b)
    is_root = sum(rel_bits) == 0
    sends = []
    for j in range(bits):
        above = sum(rel_bits[j:]) if j < bits else 0
        sends.append(above == 0)
    rows = x_ref.shape[0] // chunks

    def child(j):
        b = (me // (1 << j)) % 2
        return me + (1 - 2 * b) * (1 << j)

    def copy(c, j, src):
        part = pl.ds(c * rows, rows)
        return pltpu.make_async_remote_copy(
            src_ref=src.at[part],
            dst_ref=buf.at[part],
            send_sem=send_sem.at[c, j],
            recv_sem=recv_sem.at[c],
            device_id=(row, child(j)),
            device_id_type=pl.DeviceIdType.MESH,
        )

    for c in range(chunks):
        @pl.when(jnp.logical_not(is_root))
        def _():
            copy(c, 0, buf).wait_recv()

        for j in range(bits):
            @pl.when(sends[j] & is_root)
            def _():
                copy(c, j, x_ref).start()

            @pl.when(sends[j] & jnp.logical_not(is_root))
            def _():
                copy(c, j, buf).start()

    for c in range(chunks):
        for j in range(bits):
            @pl.when(sends[j])
            def _():
                copy(c, j, buf).wait_send()

    @pl.when(is_root)
    def _():
        y_ref[...] = x_ref[...]

    @pl.when(jnp.logical_not(is_root))
    def _():
        y_ref[...] = buf[...]


def panel_broadcast(value, size, root, chunks):
    bits = size.bit_length() - 1
    return pl.pallas_call(
        functools.partial(broadcast_kernel, root, size, chunks),
        out_shape=jax.ShapeDtypeStruct(value.shape, value.dtype),
        in_specs=[pl.BlockSpec(memory_space=pltpu.VMEM)],
        out_specs=pl.BlockSpec(memory_space=pltpu.VMEM),
        scratch_shapes=[
            pltpu.VMEM(value.shape, value.dtype),
            pltpu.SemaphoreType.DMA((chunks,)),
            pltpu.SemaphoreType.DMA((chunks, bits)),
        ],
        compiler_params=pltpu.CompilerParams(has_side_effects=True),
    )(value)


def tree_broadcast(value, axis, size, root):
    here = lax.axis_index(axis) ^ root
    step = 1
    while step < size:
        pairs = [(root ^ d, root ^ (d + step)) for d in range(step)]
        arrived = lax.ppermute(value, axis, pairs)
        take = (here >= step) & (here < 2 * step)
        value = jnp.where(take, arrived, value)
        step *= 2
    return value


def butterfly_sum(value, axis, size):
    step = 1
    while step < size:
        pairs = [(i, i ^ step) for i in range(size)]
        value = value + lax.ppermute(value, axis, pairs)
        step *= 2
    return value


def halving_scatter(value, axis, size):
    here = lax.axis_index(axis)
    band = value.shape[0] // size
    blocks = value.reshape(size, band, value.shape[1])
    step = size // 2
    while step >= 1:
        halves = blocks.reshape(2, step, band, value.shape[1])
        high = ((here // step) % 2) == 1
        keep = jnp.where(high, halves[1], halves[0])
        send = jnp.where(high, halves[0], halves[1])
        pairs = [(i, i ^ step) for i in range(size)]
        blocks = keep + lax.ppermute(send, axis, pairs)
        step //= 2
    return blocks.reshape(band, value.shape[1])


def doubling_gather(value, axis, size):
    here = lax.axis_index(axis)
    step = 1
    while step < size:
        pairs = [(i, i ^ step) for i in range(size)]
        other = lax.ppermute(value, axis, pairs)
        high = ((here // step) % 2) == 1
        value = jnp.where(
            high,
            jnp.concatenate([other, value], 0),
            jnp.concatenate([value, other], 0),
        )
        step *= 2
    return value


def halved_lower(matrix):
    order = matrix.shape[0]
    keep = jnp.tril(jnp.ones((order, order), matrix.dtype)) - 0.5 * jnp.eye(
        order, dtype=matrix.dtype
    )
    return matrix * keep


def inverse_lower(block):
    ident = jnp.eye(block.shape[0], dtype=block.dtype)
    return lax.linalg.triangular_solve(block, ident, left_side=True, lower=True)


def block_adjoint(block, inverse, seed_adj):
    inner = halved_lower(jnp.dot(block.T, seed_adj, precision=exact_mode))
    middle = jnp.dot(inverse.T, inner, precision=exact_mode)
    return halved_lower(jnp.dot(middle, inverse, precision=exact_mode))


def make_per_device(n_row, n_col):
    def per_device(
        trail,
        row_one,
        row_two,
        diag_one,
        diag_two,
        adj_trail,
        adj_row_one,
        adj_row_two,
        adj_diag_one,
        adj_diag_two,
    ):
        panel = diag_one.shape[0]
        width = trail.shape[1]
        band = row_one.shape[0]
        last = width - panel
        col_here = lax.axis_index("col")
        row_start = lax.axis_index("row") * band
        root_one = n_col - 2
        root_two = n_col - 1
        here_one = col_here == root_one
        here_two = col_here == root_two
        full_one = doubling_gather(row_one, "row", n_row)
        full_two = doubling_gather(row_two, "row", n_row)

        def own_rows(matrix):
            return lax.dynamic_slice_in_dim(matrix, row_start, band, 0)

        def solve_panel(rows, inverse, root):
            local = jnp.dot(rows, inverse, precision=exact_mode).astype(jnp.bfloat16)
            chunks = 4 if local.shape[0] % 64 == 0 else 3
            return panel_broadcast(local, n_col, root, chunks)

        def summed_block(partial_value, root):
            rows_sum = butterfly_sum(partial_value, "row", n_row)
            return tree_broadcast(rows_sum, "col", n_col, root)

        inverse_two = inverse_lower(diag_two)
        solved_two = solve_panel(adj_trail[:, last:], inverse_two, root_two)
        partial_two = jnp.dot(solved_two.T, trail[:, last:], preferred_element_type=jnp.float32)
        seed_two = jnp.tril(adj_diag_two - summed_block(partial_two, root_two))
        grad_diag_two = block_adjoint(diag_two, inverse_two, seed_two)
        mirror_two = own_rows(grad_diag_two + grad_diag_two.T)
        rest_two = jnp.dot(mirror_two, full_two.astype(jnp.float32), precision=exact_mode)
        inverse_one = inverse_lower(diag_one)
        crossed = halving_scatter(
            jnp.dot(solved_two.T, trail, preferred_element_type=jnp.float32), "row", n_row
        )
        adj_two = adj_row_two - crossed - rest_two
        adj_next = adj_trail - jnp.dot(solved_two, full_two, preferred_element_type=jnp.float32)
        stacked = jnp.concatenate([adj_two[:, last:], adj_next[:, last:]], 0)
        solved_one = solve_panel(stacked, inverse_one, root_one)
        head_rows = solved_one[:band]
        tail_rows = solved_one[band:]
        partial_one = jnp.dot(
            head_rows.T, row_two[:, last:], preferred_element_type=jnp.float32
        ) + jnp.dot(tail_rows.T, trail[:, last:], preferred_element_type=jnp.float32)
        seed_one = jnp.tril(adj_diag_one - summed_block(partial_one, root_one))
        grad_diag_one = block_adjoint(diag_one, inverse_one, seed_one)
        mirror_one = own_rows(grad_diag_one + grad_diag_one.T)
        rest_one = jnp.dot(mirror_one, full_one.astype(jnp.float32), precision=exact_mode)
        head_update = jnp.dot(head_rows, full_one, preferred_element_type=jnp.float32)
        two_left = adj_two - head_update
        trail_left = adj_next - jnp.dot(tail_rows, full_one, preferred_element_type=jnp.float32)
        crossed_one = halving_scatter(
            jnp.dot(head_rows.T, row_two, preferred_element_type=jnp.float32)
            + jnp.dot(tail_rows.T, trail, preferred_element_type=jnp.float32),
            "row",
            n_row,
        )
        one_left = adj_row_one - crossed_one - rest_one
        trail_block = jnp.where(
            here_one,
            tail_rows.astype(jnp.float32),
            jnp.where(here_two, solved_two.astype(jnp.float32), trail_left[:, last:]),
        )
        grad_trail = jnp.concatenate([trail_left[:, :last], trail_block], 1).astype(jnp.bfloat16)
        zero_block = jnp.zeros((band, panel), jnp.float32)
        one_block = jnp.where(here_one | here_two, zero_block, one_left[:, last:])
        grad_row_one = jnp.concatenate([one_left[:, :last], one_block], 1)
        two_block = jnp.where(
            here_one, head_rows.astype(jnp.float32), jnp.where(here_two, zero_block, two_left[:, last:])
        )
        grad_row_two = jnp.concatenate([two_left[:, :last], two_block], 1)
        return (grad_trail, grad_row_one, grad_row_two, grad_diag_one, grad_diag_two)

    return per_device


def solution(mesh):
    in_specs = (
        P("row", "col"),
        P("row", "col"),
        P("row", "col"),
        P(),
        P(),
        P("row", "col"),
        P("row", "col"),
        P("row", "col"),
        P(),
        P(),
    )
    out_specs = (P("row", "col"), P("row", "col"), P("row", "col"), P(), P())
    return jax.shard_map(
        make_per_device(mesh.shape["row"], mesh.shape["col"]),
        mesh=mesh,
        in_specs=in_specs,
        out_specs=out_specs,
        check_vma=False,
    )
```

```python
import functools

import jax
import jax.numpy as jnp
from jax import lax
from jax.experimental import pallas as pl
from jax.experimental.pallas import tpu as pltpu
from jax.sharding import PartitionSpec as P

exact_mode = lax.Precision.HIGHEST


def spread_kernel(root, size, x_ref, y_ref, buf, recv_sem, send_sem):
    me = lax.axis_index("col")
    row = lax.axis_index("row")
    rows = x_ref.shape[0] // size
    is_root = me == root

    def piece(p):
        return pl.ds(p * rows, rows)

    def copy(p, dest, src, phase):
        return pltpu.make_async_remote_copy(
            src_ref=src.at[piece(p)],
            dst_ref=buf.at[piece(p)],
            send_sem=send_sem.at[phase, dest],
            recv_sem=recv_sem.at[p],
            device_id=(row, dest),
            device_id_type=pl.DeviceIdType.MESH,
        )

    @pl.when(is_root)
    def _():
        for dest in range(size):
            if dest != root:
                copy(dest, dest, x_ref, 0).start()
        for dest in range(size):
            if dest != root:
                copy(root, dest, x_ref, 1).start()
        for dest in range(size):
            if dest != root:
                copy(dest, dest, x_ref, 0).wait_send()
                copy(root, dest, x_ref, 1).wait_send()
        y_ref[...] = x_ref[...]

    @pl.when(jnp.logical_not(is_root))
    def _():
        for own in range(size):
            if own == root:
                continue

            @pl.when(me == own)
            def _():
                copy(own, own, buf, 0).wait_recv()
                for dest in range(size):
                    if dest != root and dest != own:
                        copy(own, dest, buf, 1).start()
                for p in range(size):
                    if p != own:
                        copy(p, own, buf, 1).wait_recv()
                for dest in range(size):
                    if dest != root and dest != own:
                        copy(own, dest, buf, 1).wait_send()
        y_ref[...] = buf[...]


def panel_broadcast(value, size, root):
    return pl.pallas_call(
        functools.partial(spread_kernel, root, size),
        out_shape=jax.ShapeDtypeStruct(value.shape, value.dtype),
        in_specs=[pl.BlockSpec(memory_space=pltpu.VMEM)],
        out_specs=pl.BlockSpec(memory_space=pltpu.VMEM),
        scratch_shapes=[
            pltpu.VMEM(value.shape, value.dtype),
            pltpu.SemaphoreType.DMA((size,)),
            pltpu.SemaphoreType.DMA((2, size)),
        ],
        compiler_params=pltpu.CompilerParams(has_side_effects=True),
    )(value)


def tree_broadcast(value, axis, size, root):
    here = lax.axis_index(axis) ^ root
    step = 1
    while step < size:
        pairs = [(root ^ d, root ^ (d + step)) for d in range(step)]
        arrived = lax.ppermute(value, axis, pairs)
        take = (here >= step) & (here < 2 * step)
        value = jnp.where(take, arrived, value)
        step *= 2
    return value


def butterfly_sum(value, axis, size):
    step = 1
    while step < size:
        pairs = [(i, i ^ step) for i in range(size)]
        value = value + lax.ppermute(value, axis, pairs)
        step *= 2
    return value


def halving_scatter(value, axis, size):
    here = lax.axis_index(axis)
    band = value.shape[0] // size
    blocks = value.reshape(size, band, value.shape[1])
    step = size // 2
    while step >= 1:
        halves = blocks.reshape(2, step, band, value.shape[1])
        high = ((here // step) % 2) == 1
        keep = jnp.where(high, halves[1], halves[0])
        send = jnp.where(high, halves[0], halves[1])
        pairs = [(i, i ^ step) for i in range(size)]
        blocks = keep + lax.ppermute(send, axis, pairs)
        step //= 2
    return blocks.reshape(band, value.shape[1])


def doubling_gather(value, axis, size):
    here = lax.axis_index(axis)
    step = 1
    while step < size:
        pairs = [(i, i ^ step) for i in range(size)]
        other = lax.ppermute(value, axis, pairs)
        high = ((here // step) % 2) == 1
        value = jnp.where(
            high,
            jnp.concatenate([other, value], 0),
            jnp.concatenate([value, other], 0),
        )
        step *= 2
    return value


def halved_lower(matrix):
    order = matrix.shape[0]
    keep = jnp.tril(jnp.ones((order, order), matrix.dtype)) - 0.5 * jnp.eye(
        order, dtype=matrix.dtype
    )
    return matrix * keep


def inverse_lower(block):
    ident = jnp.eye(block.shape[0], dtype=block.dtype)
    return lax.linalg.triangular_solve(block, ident, left_side=True, lower=True)


def block_adjoint(block, inverse, seed_adj):
    inner = halved_lower(jnp.dot(block.T, seed_adj, precision=exact_mode))
    middle = jnp.dot(inverse.T, inner, precision=exact_mode)
    return halved_lower(jnp.dot(middle, inverse, precision=exact_mode))


def make_per_device(n_row, n_col):
    def per_device(
        trail,
        row_one,
        row_two,
        diag_one,
        diag_two,
        adj_trail,
        adj_row_one,
        adj_row_two,
        adj_diag_one,
        adj_diag_two,
    ):
        panel = diag_one.shape[0]
        width = trail.shape[1]
        band = row_one.shape[0]
        last = width - panel
        col_here = lax.axis_index("col")
        row_start = lax.axis_index("row") * band
        root_one = n_col - 2
        root_two = n_col - 1
        here_one = col_here == root_one
        here_two = col_here == root_two
        full_one = doubling_gather(row_one, "row", n_row)
        full_two = doubling_gather(row_two, "row", n_row)

        def own_rows(matrix):
            return lax.dynamic_slice_in_dim(matrix, row_start, band, 0)

        def solve_panel(rows, inverse, root):
            local = jnp.dot(rows, inverse, precision=exact_mode).astype(jnp.bfloat16)
            head = local.shape[0] % (16 * n_col)
            tail = panel_broadcast(local[head:], n_col, root)
            if head == 0:
                return tail
            return jnp.concatenate([tree_broadcast(local[:head], "col", n_col, root), tail], 0)

        def summed_block(partial_value, root):
            rows_sum = butterfly_sum(partial_value, "row", n_row)
            return tree_broadcast(rows_sum, "col", n_col, root)

        inverse_two = inverse_lower(diag_two)
        solved_two = solve_panel(adj_trail[:, last:], inverse_two, root_two)
        partial_two = jnp.dot(solved_two.T, trail[:, last:], preferred_element_type=jnp.float32)
        seed_two = jnp.tril(adj_diag_two - summed_block(partial_two, root_two))
        grad_diag_two = block_adjoint(diag_two, inverse_two, seed_two)
        mirror_two = own_rows(grad_diag_two + grad_diag_two.T)
        rest_two = jnp.dot(mirror_two, full_two.astype(jnp.float32), precision=exact_mode)
        inverse_one = inverse_lower(diag_one)
        crossed = halving_scatter(
            jnp.dot(solved_two.T, trail, preferred_element_type=jnp.float32), "row", n_row
        )
        adj_two = adj_row_two - crossed - rest_two
        adj_next = adj_trail - jnp.dot(solved_two, full_two, preferred_element_type=jnp.float32)
        stacked = jnp.concatenate([adj_two[:, last:], adj_next[:, last:]], 0)
        solved_one = solve_panel(stacked, inverse_one, root_one)
        head_rows = solved_one[:band]
        tail_rows = solved_one[band:]
        partial_one = jnp.dot(
            head_rows.T, row_two[:, last:], preferred_element_type=jnp.float32
        ) + jnp.dot(tail_rows.T, trail[:, last:], preferred_element_type=jnp.float32)
        seed_one = jnp.tril(adj_diag_one - summed_block(partial_one, root_one))
        grad_diag_one = block_adjoint(diag_one, inverse_one, seed_one)
        mirror_one = own_rows(grad_diag_one + grad_diag_one.T)
        rest_one = jnp.dot(mirror_one, full_one.astype(jnp.float32), precision=exact_mode)
        head_update = jnp.dot(head_rows, full_one, preferred_element_type=jnp.float32)
        two_left = adj_two - head_update
        trail_left = adj_next - jnp.dot(tail_rows, full_one, preferred_element_type=jnp.float32)
        crossed_one = halving_scatter(
            jnp.dot(head_rows.T, row_two, preferred_element_type=jnp.float32)
            + jnp.dot(tail_rows.T, trail, preferred_element_type=jnp.float32),
            "row",
            n_row,
        )
        one_left = adj_row_one - crossed_one - rest_one
        trail_block = jnp.where(
            here_one,
            tail_rows.astype(jnp.float32),
            jnp.where(here_two, solved_two.astype(jnp.float32), trail_left[:, last:]),
        )
        grad_trail = jnp.concatenate([trail_left[:, :last], trail_block], 1).astype(jnp.bfloat16)
        zero_block = jnp.zeros((band, panel), jnp.float32)
        one_block = jnp.where(here_one | here_two, zero_block, one_left[:, last:])
        grad_row_one = jnp.concatenate([one_left[:, :last], one_block], 1)
        two_block = jnp.where(
            here_one, head_rows.astype(jnp.float32), jnp.where(here_two, zero_block, two_left[:, last:])
        )
        grad_row_two = jnp.concatenate([two_left[:, :last], two_block], 1)
        return (grad_trail, grad_row_one, grad_row_two, grad_diag_one, grad_diag_two)

    return per_device


def solution(mesh):
    in_specs = (
        P("row", "col"),
        P("row", "col"),
        P("row", "col"),
        P(),
        P(),
        P("row", "col"),
        P("row", "col"),
        P("row", "col"),
        P(),
        P(),
    )
    out_specs = (P("row", "col"), P("row", "col"), P("row", "col"), P(), P())
    return jax.shard_map(
        make_per_device(mesh.shape["row"], mesh.shape["col"]),
        mesh=mesh,
        in_specs=in_specs,
        out_specs=out_specs,
        check_vma=False,
    )
```

```python
import functools

import jax
import jax.numpy as jnp
from jax import lax
from jax.experimental import pallas as pl
from jax.experimental.pallas import tpu as pltpu
from jax.sharding import PartitionSpec as P

exact_mode = lax.Precision.HIGHEST


def spread_kernel(root, size, x_ref, y_ref, buf, recv_sem, send_sem):
    me = lax.axis_index("col")
    row = lax.axis_index("row")
    rows = x_ref.shape[0] // size
    is_root = me == root

    def piece(p):
        return pl.ds(p * rows, rows)

    def copy(p, dest, src, phase):
        return pltpu.make_async_remote_copy(
            src_ref=src.at[piece(p)],
            dst_ref=buf.at[piece(p)],
            send_sem=send_sem.at[phase, dest],
            recv_sem=recv_sem.at[p],
            device_id=(row, dest),
            device_id_type=pl.DeviceIdType.MESH,
        )

    @pl.when(is_root)
    def _():
        for dest in range(size):
            if dest != root:
                copy(dest, dest, x_ref, 0).start()
        for dest in range(size):
            if dest != root:
                copy(root, dest, x_ref, 1).start()
        for dest in range(size):
            if dest != root:
                copy(dest, dest, x_ref, 0).wait_send()
                copy(root, dest, x_ref, 1).wait_send()
        y_ref[...] = x_ref[...]

    @pl.when(jnp.logical_not(is_root))
    def _():
        for own in range(size):
            if own == root:
                continue

            @pl.when(me == own)
            def _():
                copy(own, own, buf, 0).wait_recv()
                for dest in range(size):
                    if dest != root and dest != own:
                        copy(own, dest, buf, 1).start()
                for p in range(size):
                    if p != own:
                        copy(p, own, buf, 1).wait_recv()
                for dest in range(size):
                    if dest != root and dest != own:
                        copy(own, dest, buf, 1).wait_send()
        y_ref[...] = buf[...]


def panel_broadcast(value, size, root):
    return pl.pallas_call(
        functools.partial(spread_kernel, root, size),
        out_shape=jax.ShapeDtypeStruct(value.shape, value.dtype),
        in_specs=[pl.BlockSpec(memory_space=pltpu.VMEM)],
        out_specs=pl.BlockSpec(memory_space=pltpu.VMEM),
        scratch_shapes=[
            pltpu.VMEM(value.shape, value.dtype),
            pltpu.SemaphoreType.DMA((size,)),
            pltpu.SemaphoreType.DMA((2, size)),
        ],
        compiler_params=pltpu.CompilerParams(has_side_effects=True),
    )(value)


def tree_broadcast(value, axis, size, root):
    here = lax.axis_index(axis) ^ root
    step = 1
    while step < size:
        pairs = [(root ^ d, root ^ (d + step)) for d in range(step)]
        arrived = lax.ppermute(value, axis, pairs)
        take = (here >= step) & (here < 2 * step)
        value = jnp.where(take, arrived, value)
        step *= 2
    return value


def butterfly_sum(value, axis, size):
    step = 1
    while step < size:
        pairs = [(i, i ^ step) for i in range(size)]
        value = value + lax.ppermute(value, axis, pairs)
        step *= 2
    return value


def halving_scatter(value, axis, size):
    here = lax.axis_index(axis)
    band = value.shape[0] // size
    blocks = value.reshape(size, band, value.shape[1])
    step = size // 2
    while step >= 1:
        halves = blocks.reshape(2, step, band, value.shape[1])
        high = ((here // step) % 2) == 1
        keep = jnp.where(high, halves[1], halves[0])
        send = jnp.where(high, halves[0], halves[1])
        pairs = [(i, i ^ step) for i in range(size)]
        blocks = keep + lax.ppermute(send, axis, pairs)
        step //= 2
    return blocks.reshape(band, value.shape[1])


def doubling_gather(value, axis, size):
    here = lax.axis_index(axis)
    step = 1
    while step < size:
        pairs = [(i, i ^ step) for i in range(size)]
        other = lax.ppermute(value, axis, pairs)
        high = ((here // step) % 2) == 1
        value = jnp.where(
            high,
            jnp.concatenate([other, value], 0),
            jnp.concatenate([value, other], 0),
        )
        step *= 2
    return value


def halved_lower(matrix):
    order = matrix.shape[0]
    keep = jnp.tril(jnp.ones((order, order), matrix.dtype)) - 0.5 * jnp.eye(
        order, dtype=matrix.dtype
    )
    return matrix * keep


def inverse_lower(block):
    ident = jnp.broadcast_to(jnp.eye(block.shape[-1], dtype=block.dtype), block.shape)
    return lax.linalg.triangular_solve(block, ident, left_side=True, lower=True)


def block_adjoint(block, inverse, seed_adj):
    inner = halved_lower(jnp.dot(block.T, seed_adj, precision=exact_mode))
    middle = jnp.dot(inverse.T, inner, precision=exact_mode)
    return halved_lower(jnp.dot(middle, inverse, precision=exact_mode))


def make_per_device(n_row, n_col):
    def per_device(
        trail,
        row_one,
        row_two,
        diag_one,
        diag_two,
        adj_trail,
        adj_row_one,
        adj_row_two,
        adj_diag_one,
        adj_diag_two,
    ):
        panel = diag_one.shape[0]
        width = trail.shape[1]
        band = row_one.shape[0]
        last = width - panel
        col_here = lax.axis_index("col")
        row_start = lax.axis_index("row") * band
        root_one = n_col - 2
        root_two = n_col - 1
        here_one = col_here == root_one
        here_two = col_here == root_two
        full_one = doubling_gather(row_one, "row", n_row)
        full_two = doubling_gather(row_two, "row", n_row)

        def own_rows(matrix):
            return lax.dynamic_slice_in_dim(matrix, row_start, band, 0)

        def solve_panel(rows, inverse, root):
            local = jnp.dot(rows, inverse, precision=exact_mode).astype(jnp.bfloat16)
            head = local.shape[0] % (16 * n_col)
            tail = panel_broadcast(local[head:], n_col, root)
            if head == 0:
                return tail
            return jnp.concatenate([tree_broadcast(local[:head], "col", n_col, root), tail], 0)

        def summed_block(partial_value, root):
            rows_sum = butterfly_sum(partial_value, "row", n_row)
            return tree_broadcast(rows_sum, "col", n_col, root)

        both = inverse_lower(jnp.stack([diag_two, diag_one]))
        inverse_two = both[0]
        inverse_one = both[1]
        solved_two = solve_panel(adj_trail[:, last:], inverse_two, root_two)
        partial_two = jnp.dot(solved_two.T, trail[:, last:], preferred_element_type=jnp.float32)
        seed_two = jnp.tril(adj_diag_two - summed_block(partial_two, root_two))
        grad_diag_two = block_adjoint(diag_two, inverse_two, seed_two)
        mirror_two = own_rows(grad_diag_two + grad_diag_two.T)
        rest_two = jnp.dot(mirror_two, full_two.astype(jnp.float32), precision=exact_mode)
        crossed = halving_scatter(
            jnp.dot(solved_two.T, trail, preferred_element_type=jnp.float32), "row", n_row
        )
        adj_two = adj_row_two - crossed - rest_two
        adj_next = adj_trail - jnp.dot(solved_two, full_two, preferred_element_type=jnp.float32)
        stacked = jnp.concatenate([adj_two[:, last:], adj_next[:, last:]], 0)
        solved_one = solve_panel(stacked, inverse_one, root_one)
        head_rows = solved_one[:band]
        tail_rows = solved_one[band:]
        partial_one = jnp.dot(
            head_rows.T, row_two[:, last:], preferred_element_type=jnp.float32
        ) + jnp.dot(tail_rows.T, trail[:, last:], preferred_element_type=jnp.float32)
        seed_one = jnp.tril(adj_diag_one - summed_block(partial_one, root_one))
        grad_diag_one = block_adjoint(diag_one, inverse_one, seed_one)
        mirror_one = own_rows(grad_diag_one + grad_diag_one.T)
        rest_one = jnp.dot(mirror_one, full_one.astype(jnp.float32), precision=exact_mode)
        head_update = jnp.dot(head_rows, full_one, preferred_element_type=jnp.float32)
        two_left = adj_two - head_update
        trail_left = adj_next - jnp.dot(tail_rows, full_one, preferred_element_type=jnp.float32)
        crossed_one = halving_scatter(
            jnp.dot(head_rows.T, row_two, preferred_element_type=jnp.float32)
            + jnp.dot(tail_rows.T, trail, preferred_element_type=jnp.float32),
            "row",
            n_row,
        )
        one_left = adj_row_one - crossed_one - rest_one
        trail_block = jnp.where(
            here_one,
            tail_rows.astype(jnp.float32),
            jnp.where(here_two, solved_two.astype(jnp.float32), trail_left[:, last:]),
        )
        grad_trail = jnp.concatenate([trail_left[:, :last], trail_block], 1).astype(jnp.bfloat16)
        zero_block = jnp.zeros((band, panel), jnp.float32)
        one_block = jnp.where(here_one | here_two, zero_block, one_left[:, last:])
        grad_row_one = jnp.concatenate([one_left[:, :last], one_block], 1)
        two_block = jnp.where(
            here_one, head_rows.astype(jnp.float32), jnp.where(here_two, zero_block, two_left[:, last:])
        )
        grad_row_two = jnp.concatenate([two_left[:, :last], two_block], 1)
        return (grad_trail, grad_row_one, grad_row_two, grad_diag_one, grad_diag_two)

    return per_device


def solution(mesh):
    in_specs = (
        P("row", "col"),
        P("row", "col"),
        P("row", "col"),
        P(),
        P(),
        P("row", "col"),
        P("row", "col"),
        P("row", "col"),
        P(),
        P(),
    )
    out_specs = (P("row", "col"), P("row", "col"), P("row", "col"), P(), P())
    return jax.shard_map(
        make_per_device(mesh.shape["row"], mesh.shape["col"]),
        mesh=mesh,
        in_specs=in_specs,
        out_specs=out_specs,
        check_vma=False,
    )
```

```python
import functools

import jax
import jax.numpy as jnp
from jax import lax
from jax.experimental import pallas as pl
from jax.experimental.pallas import tpu as pltpu
from jax.sharding import PartitionSpec as P

exact_mode = lax.Precision.HIGHEST


def spread_kernel(root, size, x_ref, y_ref, buf, recv_sem, send_sem):
    me = lax.axis_index("col")
    row = lax.axis_index("row")
    rows = x_ref.shape[0] // size
    is_root = me == root

    def piece(p):
        return pl.ds(p * rows, rows)

    def copy(p, dest, src, phase):
        return pltpu.make_async_remote_copy(
            src_ref=src.at[piece(p)],
            dst_ref=buf.at[piece(p)],
            send_sem=send_sem.at[phase, dest],
            recv_sem=recv_sem.at[p],
            device_id=(row, dest),
            device_id_type=pl.DeviceIdType.MESH,
        )

    @pl.when(is_root)
    def _():
        for dest in range(size):
            if dest != root:
                copy(dest, dest, x_ref, 0).start()
        for dest in range(size):
            if dest != root:
                copy(root, dest, x_ref, 1).start()
        for dest in range(size):
            if dest != root:
                copy(dest, dest, x_ref, 0).wait_send()
                copy(root, dest, x_ref, 1).wait_send()
        y_ref[...] = x_ref[...]

    @pl.when(jnp.logical_not(is_root))
    def _():
        for own in range(size):
            if own == root:
                continue

            @pl.when(me == own)
            def _():
                copy(own, own, buf, 0).wait_recv()
                for dest in range(size):
                    if dest != root and dest != own:
                        copy(own, dest, buf, 1).start()
                for p in range(size):
                    if p != own:
                        copy(p, own, buf, 1).wait_recv()
                for dest in range(size):
                    if dest != root and dest != own:
                        copy(own, dest, buf, 1).wait_send()
        y_ref[...] = buf[...]


def panel_broadcast(value, size, root):
    return pl.pallas_call(
        functools.partial(spread_kernel, root, size),
        out_shape=jax.ShapeDtypeStruct(value.shape, value.dtype),
        in_specs=[pl.BlockSpec(memory_space=pltpu.VMEM)],
        out_specs=pl.BlockSpec(memory_space=pltpu.VMEM),
        scratch_shapes=[
            pltpu.VMEM(value.shape, value.dtype),
            pltpu.SemaphoreType.DMA((size,)),
            pltpu.SemaphoreType.DMA((2, size)),
        ],
        compiler_params=pltpu.CompilerParams(has_side_effects=True),
    )(value)


def tree_broadcast(value, axis, size, root):
    here = lax.axis_index(axis) ^ root
    step = 1
    while step < size:
        pairs = [(root ^ d, root ^ (d + step)) for d in range(step)]
        arrived = lax.ppermute(value, axis, pairs)
        take = (here >= step) & (here < 2 * step)
        value = jnp.where(take, arrived, value)
        step *= 2
    return value


def butterfly_sum(value, axis, size):
    step = 1
    while step < size:
        pairs = [(i, i ^ step) for i in range(size)]
        value = value + lax.ppermute(value, axis, pairs)
        step *= 2
    return value


def halving_scatter(value, axis, size):
    here = lax.axis_index(axis)
    band = value.shape[0] // size
    blocks = value.reshape(size, band, value.shape[1])
    step = size // 2
    while step >= 1:
        halves = blocks.reshape(2, step, band, value.shape[1])
        high = ((here // step) % 2) == 1
        keep = jnp.where(high, halves[1], halves[0])
        send = jnp.where(high, halves[0], halves[1])
        pairs = [(i, i ^ step) for i in range(size)]
        blocks = keep + lax.ppermute(send, axis, pairs)
        step //= 2
    return blocks.reshape(band, value.shape[1])


def doubling_gather(value, axis, size):
    here = lax.axis_index(axis)
    step = 1
    while step < size:
        pairs = [(i, i ^ step) for i in range(size)]
        other = lax.ppermute(value, axis, pairs)
        high = ((here // step) % 2) == 1
        value = jnp.where(
            high,
            jnp.concatenate([other, value], 0),
            jnp.concatenate([value, other], 0),
        )
        step *= 2
    return value


def halved_lower(matrix):
    order = matrix.shape[0]
    keep = jnp.tril(jnp.ones((order, order), matrix.dtype)) - 0.5 * jnp.eye(
        order, dtype=matrix.dtype
    )
    return matrix * keep


def inverse_lower(block):
    ident = jnp.eye(block.shape[0], dtype=block.dtype)
    return lax.linalg.triangular_solve(block, ident, left_side=True, lower=True)


def block_adjoint(block, inverse, seed_adj):
    inner = halved_lower(jnp.dot(block.T, seed_adj, precision=exact_mode))
    middle = jnp.dot(inverse.T, inner, precision=exact_mode)
    return halved_lower(jnp.dot(middle, inverse, precision=exact_mode))


def make_per_device(n_row, n_col):
    def per_device(
        trail,
        row_one,
        row_two,
        diag_one,
        diag_two,
        adj_trail,
        adj_row_one,
        adj_row_two,
        adj_diag_one,
        adj_diag_two,
    ):
        panel = diag_one.shape[0]
        width = trail.shape[1]
        band = row_one.shape[0]
        last = width - panel
        col_here = lax.axis_index("col")
        row_start = lax.axis_index("row") * band
        root_one = n_col - 2
        root_two = n_col - 1
        here_one = col_here == root_one
        here_two = col_here == root_two
        full_one = doubling_gather(row_one, "row", n_row)
        full_two = doubling_gather(row_two, "row", n_row)

        def own_rows(matrix):
            return lax.dynamic_slice_in_dim(matrix, row_start, band, 0)

        def solve_panel(rows, inverse, root):
            local = jnp.dot(rows, inverse, precision=exact_mode).astype(jnp.bfloat16)
            head = local.shape[0] % (16 * n_col)
            tail = panel_broadcast(local[head:], n_col, root)
            if head == 0:
                return tail
            return jnp.concatenate([tree_broadcast(local[:head], "col", n_col, root), tail], 0)

        def summed_block(partial_value, root):
            rows_sum = butterfly_sum(partial_value, "row", n_row)
            return panel_broadcast(rows_sum, n_col, root)

        inverse_two = inverse_lower(diag_two)
        solved_two = solve_panel(adj_trail[:, last:], inverse_two, root_two)
        partial_two = jnp.dot(solved_two.T, trail[:, last:], preferred_element_type=jnp.float32)
        seed_two = jnp.tril(adj_diag_two - summed_block(partial_two, root_two))
        grad_diag_two = block_adjoint(diag_two, inverse_two, seed_two)
        mirror_two = own_rows(grad_diag_two + grad_diag_two.T)
        rest_two = jnp.dot(mirror_two, full_two.astype(jnp.float32), precision=exact_mode)
        inverse_one = inverse_lower(diag_one)
        crossed = halving_scatter(
            jnp.dot(solved_two.T, trail, preferred_element_type=jnp.float32), "row", n_row
        )
        adj_two = adj_row_two - crossed - rest_two
        adj_next = adj_trail - jnp.dot(solved_two, full_two, preferred_element_type=jnp.float32)
        stacked = jnp.concatenate([adj_two[:, last:], adj_next[:, last:]], 0)
        solved_one = solve_panel(stacked, inverse_one, root_one)
        head_rows = solved_one[:band]
        tail_rows = solved_one[band:]
        partial_one = jnp.dot(
            head_rows.T, row_two[:, last:], preferred_element_type=jnp.float32
        ) + jnp.dot(tail_rows.T, trail[:, last:], preferred_element_type=jnp.float32)
        seed_one = jnp.tril(adj_diag_one - summed_block(partial_one, root_one))
        grad_diag_one = block_adjoint(diag_one, inverse_one, seed_one)
        mirror_one = own_rows(grad_diag_one + grad_diag_one.T)
        rest_one = jnp.dot(mirror_one, full_one.astype(jnp.float32), precision=exact_mode)
        head_update = jnp.dot(head_rows, full_one, preferred_element_type=jnp.float32)
        two_left = adj_two - head_update
        trail_left = adj_next - jnp.dot(tail_rows, full_one, preferred_element_type=jnp.float32)
        crossed_one = halving_scatter(
            jnp.dot(head_rows.T, row_two, preferred_element_type=jnp.float32)
            + jnp.dot(tail_rows.T, trail, preferred_element_type=jnp.float32),
            "row",
            n_row,
        )
        one_left = adj_row_one - crossed_one - rest_one
        trail_block = jnp.where(
            here_one,
            tail_rows.astype(jnp.float32),
            jnp.where(here_two, solved_two.astype(jnp.float32), trail_left[:, last:]),
        )
        grad_trail = jnp.concatenate([trail_left[:, :last], trail_block], 1).astype(jnp.bfloat16)
        zero_block = jnp.zeros((band, panel), jnp.float32)
        one_block = jnp.where(here_one | here_two, zero_block, one_left[:, last:])
        grad_row_one = jnp.concatenate([one_left[:, :last], one_block], 1)
        two_block = jnp.where(
            here_one, head_rows.astype(jnp.float32), jnp.where(here_two, zero_block, two_left[:, last:])
        )
        grad_row_two = jnp.concatenate([two_left[:, :last], two_block], 1)
        return (grad_trail, grad_row_one, grad_row_two, grad_diag_one, grad_diag_two)

    return per_device


def solution(mesh):
    in_specs = (
        P("row", "col"),
        P("row", "col"),
        P("row", "col"),
        P(),
        P(),
        P("row", "col"),
        P("row", "col"),
        P("row", "col"),
        P(),
        P(),
    )
    out_specs = (P("row", "col"), P("row", "col"), P("row", "col"), P(), P())
    return jax.shard_map(
        make_per_device(mesh.shape["row"], mesh.shape["col"]),
        mesh=mesh,
        in_specs=in_specs,
        out_specs=out_specs,
        check_vma=False,
    )
```

```python
import functools

import jax
import jax.numpy as jnp
from jax import lax
from jax.experimental import pallas as pl
from jax.experimental.pallas import tpu as pltpu
from jax.sharding import PartitionSpec as P

exact_mode = lax.Precision.HIGHEST


def spread_kernel(root, size, x_ref, y_ref, buf, recv_sem, send_sem):
    me = lax.axis_index("col")
    row = lax.axis_index("row")
    barrier = pltpu.get_barrier_semaphore()
    for step in range(1, size):
        pl.semaphore_signal(
            barrier,
            inc=1,
            device_id=(row, lax.rem(me + step, size)),
            device_id_type=pl.DeviceIdType.MESH,
        )
    pl.semaphore_wait(barrier, size - 1)
    rows = x_ref.shape[0] // size
    is_root = me == root

    def piece(p):
        return pl.ds(p * rows, rows)

    def copy(p, dest, src, phase):
        return pltpu.make_async_remote_copy(
            src_ref=src.at[piece(p)],
            dst_ref=buf.at[piece(p)],
            send_sem=send_sem.at[phase, dest],
            recv_sem=recv_sem.at[p],
            device_id=(row, dest),
            device_id_type=pl.DeviceIdType.MESH,
        )

    @pl.when(is_root)
    def _():
        for dest in range(size):
            if dest != root:
                copy(dest, dest, x_ref, 0).start()
        for dest in range(size):
            if dest != root:
                copy(root, dest, x_ref, 1).start()
        for dest in range(size):
            if dest != root:
                copy(dest, dest, x_ref, 0).wait_send()
                copy(root, dest, x_ref, 1).wait_send()
        y_ref[...] = x_ref[...]

    @pl.when(jnp.logical_not(is_root))
    def _():
        for own in range(size):
            if own == root:
                continue

            @pl.when(me == own)
            def _():
                copy(own, own, buf, 0).wait_recv()
                for dest in range(size):
                    if dest != root and dest != own:
                        copy(own, dest, buf, 1).start()
                for p in range(size):
                    if p != own:
                        copy(p, own, buf, 1).wait_recv()
                for dest in range(size):
                    if dest != root and dest != own:
                        copy(own, dest, buf, 1).wait_send()
        y_ref[...] = buf[...]


def panel_broadcast(value, size, root, call_id):
    return pl.pallas_call(
        functools.partial(spread_kernel, root, size),
        out_shape=jax.ShapeDtypeStruct(value.shape, value.dtype),
        in_specs=[pl.BlockSpec(memory_space=pltpu.VMEM)],
        out_specs=pl.BlockSpec(memory_space=pltpu.VMEM),
        scratch_shapes=[
            pltpu.VMEM(value.shape, value.dtype),
            pltpu.SemaphoreType.DMA((size,)),
            pltpu.SemaphoreType.DMA((2, size)),
        ],
        compiler_params=pltpu.CompilerParams(collective_id=call_id, has_side_effects=True),
    )(value)


def tree_broadcast(value, axis, size, root):
    here = lax.axis_index(axis) ^ root
    step = 1
    while step < size:
        pairs = [(root ^ d, root ^ (d + step)) for d in range(step)]
        arrived = lax.ppermute(value, axis, pairs)
        take = (here >= step) & (here < 2 * step)
        value = jnp.where(take, arrived, value)
        step *= 2
    return value


def butterfly_sum(value, axis, size):
    step = 1
    while step < size:
        pairs = [(i, i ^ step) for i in range(size)]
        value = value + lax.ppermute(value, axis, pairs)
        step *= 2
    return value


def halving_scatter(value, axis, size):
    here = lax.axis_index(axis)
    band = value.shape[0] // size
    blocks = value.reshape(size, band, value.shape[1])
    step = size // 2
    while step >= 1:
        halves = blocks.reshape(2, step, band, value.shape[1])
        high = ((here // step) % 2) == 1
        keep = jnp.where(high, halves[1], halves[0])
        send = jnp.where(high, halves[0], halves[1])
        pairs = [(i, i ^ step) for i in range(size)]
        blocks = keep + lax.ppermute(send, axis, pairs)
        step //= 2
    return blocks.reshape(band, value.shape[1])


def doubling_gather(value, axis, size):
    here = lax.axis_index(axis)
    step = 1
    while step < size:
        pairs = [(i, i ^ step) for i in range(size)]
        other = lax.ppermute(value, axis, pairs)
        high = ((here // step) % 2) == 1
        value = jnp.where(
            high,
            jnp.concatenate([other, value], 0),
            jnp.concatenate([value, other], 0),
        )
        step *= 2
    return value


def halved_lower(matrix):
    order = matrix.shape[0]
    keep = jnp.tril(jnp.ones((order, order), matrix.dtype)) - 0.5 * jnp.eye(
        order, dtype=matrix.dtype
    )
    return matrix * keep


def inverse_lower(block):
    ident = jnp.eye(block.shape[0], dtype=block.dtype)
    return lax.linalg.triangular_solve(block, ident, left_side=True, lower=True)


def block_adjoint(block, inverse, seed_adj):
    inner = halved_lower(jnp.dot(block.T, seed_adj, precision=exact_mode))
    middle = jnp.dot(inverse.T, inner, precision=exact_mode)
    return halved_lower(jnp.dot(middle, inverse, precision=exact_mode))


def make_per_device(n_row, n_col):
    def per_device(
        trail,
        row_one,
        row_two,
        diag_one,
        diag_two,
        adj_trail,
        adj_row_one,
        adj_row_two,
        adj_diag_one,
        adj_diag_two,
    ):
        panel = diag_one.shape[0]
        width = trail.shape[1]
        band = row_one.shape[0]
        last = width - panel
        col_here = lax.axis_index("col")
        row_start = lax.axis_index("row") * band
        root_one = n_col - 2
        root_two = n_col - 1
        here_one = col_here == root_one
        here_two = col_here == root_two
        full_one = doubling_gather(row_one, "row", n_row)
        full_two = doubling_gather(row_two, "row", n_row)

        def own_rows(matrix):
            return lax.dynamic_slice_in_dim(matrix, row_start, band, 0)

        def solve_panel(rows, inverse, root):
            local = jnp.dot(rows, inverse, precision=exact_mode).astype(jnp.bfloat16)
            head = local.shape[0] % (16 * n_col)
            tail = panel_broadcast(local[head:], n_col, root, n_col - 1 - root)
            if head == 0:
                return tail
            return jnp.concatenate([tree_broadcast(local[:head], "col", n_col, root), tail], 0)

        def summed_block(partial_value, root):
            rows_sum = butterfly_sum(partial_value, "row", n_row)
            return tree_broadcast(rows_sum, "col", n_col, root)

        inverse_two = inverse_lower(diag_two)
        solved_two = solve_panel(adj_trail[:, last:], inverse_two, root_two)
        partial_two = jnp.dot(solved_two.T, trail[:, last:], preferred_element_type=jnp.float32)
        seed_two = jnp.tril(adj_diag_two - summed_block(partial_two, root_two))
        grad_diag_two = block_adjoint(diag_two, inverse_two, seed_two)
        mirror_two = own_rows(grad_diag_two + grad_diag_two.T)
        rest_two = jnp.dot(mirror_two, full_two.astype(jnp.float32), precision=exact_mode)
        inverse_one = inverse_lower(diag_one)
        crossed = halving_scatter(
            jnp.dot(solved_two.T, trail, preferred_element_type=jnp.float32), "row", n_row
        )
        adj_two = adj_row_two - crossed - rest_two
        adj_next = adj_trail - jnp.dot(solved_two, full_two, preferred_element_type=jnp.float32)
        stacked = jnp.concatenate([adj_two[:, last:], adj_next[:, last:]], 0)
        solved_one = solve_panel(stacked, inverse_one, root_one)
        head_rows = solved_one[:band]
        tail_rows = solved_one[band:]
        partial_one = jnp.dot(
            head_rows.T, row_two[:, last:], preferred_element_type=jnp.float32
        ) + jnp.dot(tail_rows.T, trail[:, last:], preferred_element_type=jnp.float32)
        seed_one = jnp.tril(adj_diag_one - summed_block(partial_one, root_one))
        grad_diag_one = block_adjoint(diag_one, inverse_one, seed_one)
        mirror_one = own_rows(grad_diag_one + grad_diag_one.T)
        rest_one = jnp.dot(mirror_one, full_one.astype(jnp.float32), precision=exact_mode)
        head_update = jnp.dot(head_rows, full_one, preferred_element_type=jnp.float32)
        two_left = adj_two - head_update
        trail_left = adj_next - jnp.dot(tail_rows, full_one, preferred_element_type=jnp.float32)
        crossed_one = halving_scatter(
            jnp.dot(head_rows.T, row_two, preferred_element_type=jnp.float32)
            + jnp.dot(tail_rows.T, trail, preferred_element_type=jnp.float32),
            "row",
            n_row,
        )
        one_left = adj_row_one - crossed_one - rest_one
        trail_block = jnp.where(
            here_one,
            tail_rows.astype(jnp.float32),
            jnp.where(here_two, solved_two.astype(jnp.float32), trail_left[:, last:]),
        )
        grad_trail = jnp.concatenate([trail_left[:, :last], trail_block], 1).astype(jnp.bfloat16)
        zero_block = jnp.zeros((band, panel), jnp.float32)
        one_block = jnp.where(here_one | here_two, zero_block, one_left[:, last:])
        grad_row_one = jnp.concatenate([one_left[:, :last], one_block], 1)
        two_block = jnp.where(
            here_one, head_rows.astype(jnp.float32), jnp.where(here_two, zero_block, two_left[:, last:])
        )
        grad_row_two = jnp.concatenate([two_left[:, :last], two_block], 1)
        return (grad_trail, grad_row_one, grad_row_two, grad_diag_one, grad_diag_two)

    return per_device


def solution(mesh):
    in_specs = (
        P("row", "col"),
        P("row", "col"),
        P("row", "col"),
        P(),
        P(),
        P("row", "col"),
        P("row", "col"),
        P("row", "col"),
        P(),
        P(),
    )
    out_specs = (P("row", "col"), P("row", "col"), P("row", "col"), P(), P())
    return jax.shard_map(
        make_per_device(mesh.shape["row"], mesh.shape["col"]),
        mesh=mesh,
        in_specs=in_specs,
        out_specs=out_specs,
        check_vma=False,
    )
```

```python
import functools

import jax
import jax.numpy as jnp
from jax import lax
from jax.experimental import pallas as pl
from jax.experimental.pallas import tpu as pltpu
from jax.sharding import PartitionSpec as P

exact_mode = lax.Precision.HIGHEST


def spread_kernel(root, size, x_ref, y_ref, buf, recv_sem, send_sem):
    me = lax.axis_index("col")
    row = lax.axis_index("row")
    barrier = pltpu.get_barrier_semaphore()
    for step in range(1, size):
        pl.semaphore_signal(
            barrier,
            inc=1,
            device_id=(row, lax.rem(me + step, size)),
            device_id_type=pl.DeviceIdType.MESH,
        )
    pl.semaphore_wait(barrier, size - 1)
    rows = x_ref.shape[0] // size
    is_root = me == root

    def piece(p):
        return pl.ds(p * rows, rows)

    def copy(p, dest, src, phase):
        return pltpu.make_async_remote_copy(
            src_ref=src.at[piece(p)],
            dst_ref=buf.at[piece(p)],
            send_sem=send_sem.at[phase, dest],
            recv_sem=recv_sem.at[p],
            device_id=(row, dest),
            device_id_type=pl.DeviceIdType.MESH,
        )

    @pl.when(is_root)
    def _():
        for dest in range(size):
            if dest != root:
                copy(dest, dest, x_ref, 0).start()
        for dest in range(size):
            if dest != root:
                copy(root, dest, x_ref, 1).start()
        for dest in range(size):
            if dest != root:
                copy(dest, dest, x_ref, 0).wait_send()
                copy(root, dest, x_ref, 1).wait_send()
        y_ref[...] = x_ref[...]

    @pl.when(jnp.logical_not(is_root))
    def _():
        for own in range(size):
            if own == root:
                continue

            @pl.when(me == own)
            def _():
                copy(own, own, buf, 0).wait_recv()
                for dest in range(size):
                    if dest != root and dest != own:
                        copy(own, dest, buf, 1).start()
                for p in range(size):
                    if p != own:
                        copy(p, own, buf, 1).wait_recv()
                for dest in range(size):
                    if dest != root and dest != own:
                        copy(own, dest, buf, 1).wait_send()
        y_ref[...] = buf[...]


def panel_broadcast(value, size, root, call_id):
    return pl.pallas_call(
        functools.partial(spread_kernel, root, size),
        out_shape=jax.ShapeDtypeStruct(value.shape, value.dtype),
        in_specs=[pl.BlockSpec(memory_space=pltpu.VMEM)],
        out_specs=pl.BlockSpec(memory_space=pltpu.VMEM),
        scratch_shapes=[
            pltpu.VMEM(value.shape, value.dtype),
            pltpu.SemaphoreType.DMA((size,)),
            pltpu.SemaphoreType.DMA((2, size)),
        ],
        compiler_params=pltpu.CompilerParams(collective_id=call_id, has_side_effects=True),
    )(value)


def tree_broadcast(value, axis, size, root):
    here = lax.axis_index(axis) ^ root
    step = 1
    while step < size:
        pairs = [(root ^ d, root ^ (d + step)) for d in range(step)]
        arrived = lax.ppermute(value, axis, pairs)
        take = (here >= step) & (here < 2 * step)
        value = jnp.where(take, arrived, value)
        step *= 2
    return value


def butterfly_sum(value, axis, size):
    step = 1
    while step < size:
        pairs = [(i, i ^ step) for i in range(size)]
        value = value + lax.ppermute(value, axis, pairs)
        step *= 2
    return value


def halving_scatter(value, axis, size):
    here = lax.axis_index(axis)
    band = value.shape[0] // size
    blocks = value.reshape(size, band, value.shape[1])
    step = size // 2
    while step >= 1:
        halves = blocks.reshape(2, step, band, value.shape[1])
        high = ((here // step) % 2) == 1
        keep = jnp.where(high, halves[1], halves[0])
        send = jnp.where(high, halves[0], halves[1])
        pairs = [(i, i ^ step) for i in range(size)]
        blocks = keep + lax.ppermute(send, axis, pairs)
        step //= 2
    return blocks.reshape(band, value.shape[1])


def doubling_gather(value, axis, size):
    here = lax.axis_index(axis)
    step = 1
    while step < size:
        pairs = [(i, i ^ step) for i in range(size)]
        other = lax.ppermute(value, axis, pairs)
        high = ((here // step) % 2) == 1
        value = jnp.where(
            high,
            jnp.concatenate([other, value], 0),
            jnp.concatenate([value, other], 0),
        )
        step *= 2
    return value


def halved_lower(matrix):
    order = matrix.shape[0]
    keep = jnp.tril(jnp.ones((order, order), matrix.dtype)) - 0.5 * jnp.eye(
        order, dtype=matrix.dtype
    )
    return matrix * keep


def inverse_lower(block):
    ident = jnp.eye(block.shape[0], dtype=block.dtype)
    return lax.linalg.triangular_solve(block, ident, left_side=True, lower=True)


def block_adjoint(block, inverse, seed_adj):
    inner = halved_lower(jnp.dot(block.T, seed_adj, precision=exact_mode))
    middle = jnp.dot(inverse.T, inner, precision=exact_mode)
    return halved_lower(jnp.dot(middle, inverse, precision=exact_mode))


def make_per_device(n_row, n_col):
    def per_device(
        trail,
        row_one,
        row_two,
        diag_one,
        diag_two,
        adj_trail,
        adj_row_one,
        adj_row_two,
        adj_diag_one,
        adj_diag_two,
    ):
        panel = diag_one.shape[0]
        width = trail.shape[1]
        band = row_one.shape[0]
        last = width - panel
        col_here = lax.axis_index("col")
        row_start = lax.axis_index("row") * band
        root_one = n_col - 2
        root_two = n_col - 1
        here_one = col_here == root_one
        here_two = col_here == root_two
        full_one = doubling_gather(row_one, "row", n_row)
        full_two = doubling_gather(row_two, "row", n_row)

        def own_rows(matrix):
            return lax.dynamic_slice_in_dim(matrix, row_start, band, 0)

        def solve_panel(rows, inverse, root):
            local = jnp.dot(rows, inverse, precision=exact_mode).astype(jnp.bfloat16)
            head = local.shape[0] % (16 * n_col)
            tail = panel_broadcast(local[head:], n_col, root, n_col - 1 - root)
            if head == 0:
                return tail
            return jnp.concatenate([tree_broadcast(local[:head], "col", n_col, root), tail], 0)

        def summed_block(partial_value, root):
            rows_sum = butterfly_sum(partial_value, "row", n_row)
            return tree_broadcast(rows_sum, "col", n_col, root)

        inverse_two = inverse_lower(diag_two)
        solved_two = solve_panel(adj_trail[:, last:], inverse_two, root_two)
        partial_two = jnp.dot(solved_two.T, trail[:, last:], preferred_element_type=jnp.float32)
        rows_two = butterfly_sum(partial_two, "row", n_row)
        diag_one_late, rows_two = lax.optimization_barrier((diag_one, rows_two))
        inverse_one = inverse_lower(diag_one_late)
        seed_two = jnp.tril(adj_diag_two - tree_broadcast(rows_two, "col", n_col, root_two))
        grad_diag_two = block_adjoint(diag_two, inverse_two, seed_two)
        mirror_two = own_rows(grad_diag_two + grad_diag_two.T)
        rest_two = jnp.dot(mirror_two, full_two.astype(jnp.float32), precision=exact_mode)
        crossed = halving_scatter(
            jnp.dot(solved_two.T, trail, preferred_element_type=jnp.float32), "row", n_row
        )
        adj_two = adj_row_two - crossed - rest_two
        adj_next = adj_trail - jnp.dot(solved_two, full_two, preferred_element_type=jnp.float32)
        stacked = jnp.concatenate([adj_two[:, last:], adj_next[:, last:]], 0)
        solved_one = solve_panel(stacked, inverse_one, root_one)
        head_rows = solved_one[:band]
        tail_rows = solved_one[band:]
        partial_one = jnp.dot(
            head_rows.T, row_two[:, last:], preferred_element_type=jnp.float32
        ) + jnp.dot(tail_rows.T, trail[:, last:], preferred_element_type=jnp.float32)
        seed_one = jnp.tril(adj_diag_one - summed_block(partial_one, root_one))
        grad_diag_one = block_adjoint(diag_one, inverse_one, seed_one)
        mirror_one = own_rows(grad_diag_one + grad_diag_one.T)
        rest_one = jnp.dot(mirror_one, full_one.astype(jnp.float32), precision=exact_mode)
        head_update = jnp.dot(head_rows, full_one, preferred_element_type=jnp.float32)
        two_left = adj_two - head_update
        trail_left = adj_next - jnp.dot(tail_rows, full_one, preferred_element_type=jnp.float32)
        crossed_one = halving_scatter(
            jnp.dot(head_rows.T, row_two, preferred_element_type=jnp.float32)
            + jnp.dot(tail_rows.T, trail, preferred_element_type=jnp.float32),
            "row",
            n_row,
        )
        one_left = adj_row_one - crossed_one - rest_one
        trail_block = jnp.where(
            here_one,
            tail_rows.astype(jnp.float32),
            jnp.where(here_two, solved_two.astype(jnp.float32), trail_left[:, last:]),
        )
        grad_trail = jnp.concatenate([trail_left[:, :last], trail_block], 1).astype(jnp.bfloat16)
        zero_block = jnp.zeros((band, panel), jnp.float32)
        one_block = jnp.where(here_one | here_two, zero_block, one_left[:, last:])
        grad_row_one = jnp.concatenate([one_left[:, :last], one_block], 1)
        two_block = jnp.where(
            here_one, head_rows.astype(jnp.float32), jnp.where(here_two, zero_block, two_left[:, last:])
        )
        grad_row_two = jnp.concatenate([two_left[:, :last], two_block], 1)
        return (grad_trail, grad_row_one, grad_row_two, grad_diag_one, grad_diag_two)

    return per_device


def solution(mesh):
    in_specs = (
        P("row", "col"),
        P("row", "col"),
        P("row", "col"),
        P(),
        P(),
        P("row", "col"),
        P("row", "col"),
        P("row", "col"),
        P(),
        P(),
    )
    out_specs = (P("row", "col"), P("row", "col"), P("row", "col"), P(), P())
    return jax.shard_map(
        make_per_device(mesh.shape["row"], mesh.shape["col"]),
        mesh=mesh,
        in_specs=in_specs,
        out_specs=out_specs,
        check_vma=False,
    )
```

```python
import functools

import jax
import jax.numpy as jnp
from jax import lax
from jax.experimental import pallas as pl
from jax.experimental.pallas import tpu as pltpu
from jax.sharding import PartitionSpec as P

exact_mode = lax.Precision.HIGHEST


def spread_kernel(root, size, x_ref, y_ref, buf, recv_sem, send_sem):
    me = lax.axis_index("col")
    row = lax.axis_index("row")
    barrier = pltpu.get_barrier_semaphore()
    for step in range(1, size):
        pl.semaphore_signal(
            barrier,
            inc=1,
            device_id=(row, lax.rem(me + step, size)),
            device_id_type=pl.DeviceIdType.MESH,
        )
    pl.semaphore_wait(barrier, size - 1)
    rows = x_ref.shape[0] // size
    is_root = me == root

    def piece(p):
        return pl.ds(p * rows, rows)

    def copy(p, dest, src, phase):
        return pltpu.make_async_remote_copy(
            src_ref=src.at[piece(p)],
            dst_ref=buf.at[piece(p)],
            send_sem=send_sem.at[phase, dest],
            recv_sem=recv_sem.at[p],
            device_id=(row, dest),
            device_id_type=pl.DeviceIdType.MESH,
        )

    @pl.when(is_root)
    def _():
        for dest in range(size):
            if dest != root:
                copy(dest, dest, x_ref, 0).start()
        for dest in range(size):
            if dest != root:
                copy(root, dest, x_ref, 1).start()
        for dest in range(size):
            if dest != root:
                copy(dest, dest, x_ref, 0).wait_send()
                copy(root, dest, x_ref, 1).wait_send()
        y_ref[...] = x_ref[...]

    @pl.when(jnp.logical_not(is_root))
    def _():
        for own in range(size):
            if own == root:
                continue

            @pl.when(me == own)
            def _():
                copy(own, own, buf, 0).wait_recv()
                for dest in range(size):
                    if dest != root and dest != own:
                        copy(own, dest, buf, 1).start()
                for p in range(size):
                    if p != own:
                        copy(p, own, buf, 1).wait_recv()
                for dest in range(size):
                    if dest != root and dest != own:
                        copy(own, dest, buf, 1).wait_send()
        y_ref[...] = buf[...]


def panel_broadcast(value, size, root, call_id):
    return pl.pallas_call(
        functools.partial(spread_kernel, root, size),
        out_shape=jax.ShapeDtypeStruct(value.shape, value.dtype),
        in_specs=[pl.BlockSpec(memory_space=pltpu.VMEM)],
        out_specs=pl.BlockSpec(memory_space=pltpu.VMEM),
        scratch_shapes=[
            pltpu.VMEM(value.shape, value.dtype),
            pltpu.SemaphoreType.DMA((size,)),
            pltpu.SemaphoreType.DMA((2, size)),
        ],
        compiler_params=pltpu.CompilerParams(collective_id=call_id, has_side_effects=True),
    )(value)


def tree_broadcast(value, axis, size, root):
    here = lax.axis_index(axis) ^ root
    step = 1
    while step < size:
        pairs = [(root ^ d, root ^ (d + step)) for d in range(step)]
        arrived = lax.ppermute(value, axis, pairs)
        take = (here >= step) & (here < 2 * step)
        value = jnp.where(take, arrived, value)
        step *= 2
    return value


def butterfly_sum(value, axis, size):
    step = 1
    while step < size:
        pairs = [(i, i ^ step) for i in range(size)]
        value = value + lax.ppermute(value, axis, pairs)
        step *= 2
    return value


def halving_scatter(value, axis, size):
    here = lax.axis_index(axis)
    band = value.shape[0] // size
    blocks = value.reshape(size, band, value.shape[1])
    step = size // 2
    while step >= 1:
        halves = blocks.reshape(2, step, band, value.shape[1])
        high = ((here // step) % 2) == 1
        keep = jnp.where(high, halves[1], halves[0])
        send = jnp.where(high, halves[0], halves[1])
        pairs = [(i, i ^ step) for i in range(size)]
        blocks = keep + lax.ppermute(send, axis, pairs)
        step //= 2
    return blocks.reshape(band, value.shape[1])


def doubling_gather(value, axis, size):
    here = lax.axis_index(axis)
    step = 1
    while step < size:
        pairs = [(i, i ^ step) for i in range(size)]
        other = lax.ppermute(value, axis, pairs)
        high = ((here // step) % 2) == 1
        value = jnp.where(
            high,
            jnp.concatenate([other, value], 0),
            jnp.concatenate([value, other], 0),
        )
        step *= 2
    return value


def halved_lower(matrix):
    order = matrix.shape[0]
    keep = jnp.tril(jnp.ones((order, order), matrix.dtype)) - 0.5 * jnp.eye(
        order, dtype=matrix.dtype
    )
    return matrix * keep


def inverse_lower(block):
    ident = jnp.eye(block.shape[0], dtype=block.dtype)
    return lax.linalg.triangular_solve(block, ident, left_side=True, lower=True)


def block_adjoint(block, inverse, seed_adj):
    inner = halved_lower(jnp.dot(block.T, seed_adj, precision=exact_mode))
    middle = jnp.dot(inverse.T, inner, precision=exact_mode)
    return halved_lower(jnp.dot(middle, inverse, precision=exact_mode))


def make_per_device(n_row, n_col):
    def per_device(
        trail,
        row_one,
        row_two,
        diag_one,
        diag_two,
        adj_trail,
        adj_row_one,
        adj_row_two,
        adj_diag_one,
        adj_diag_two,
    ):
        panel = diag_one.shape[0]
        width = trail.shape[1]
        band = row_one.shape[0]
        last = width - panel
        col_here = lax.axis_index("col")
        row_start = lax.axis_index("row") * band
        root_one = n_col - 2
        root_two = n_col - 1
        here_one = col_here == root_one
        here_two = col_here == root_two
        full_one = doubling_gather(row_one, "row", n_row)
        full_two = doubling_gather(row_two, "row", n_row)

        def own_rows(matrix):
            return lax.dynamic_slice_in_dim(matrix, row_start, band, 0)

        def solve_panel(rows, inverse, root):
            local = jnp.dot(rows, inverse, precision=exact_mode).astype(jnp.bfloat16)
            head = local.shape[0] % (16 * n_col)
            tail = panel_broadcast(local[head:], n_col, root, n_col - 1 - root)
            if head == 0:
                return tail
            return jnp.concatenate([tree_broadcast(local[:head], "col", n_col, root), tail], 0)

        def summed_block(partial_value, root):
            rows_sum = butterfly_sum(partial_value, "row", n_row)
            return panel_broadcast(rows_sum, n_col, root, n_col + 1 - root)

        inverse_two = inverse_lower(diag_two)
        solved_two = solve_panel(adj_trail[:, last:], inverse_two, root_two)
        partial_two = jnp.dot(solved_two.T, trail[:, last:], preferred_element_type=jnp.float32)
        seed_two = jnp.tril(adj_diag_two - summed_block(partial_two, root_two))
        grad_diag_two = block_adjoint(diag_two, inverse_two, seed_two)
        mirror_two = own_rows(grad_diag_two + grad_diag_two.T)
        rest_two = jnp.dot(mirror_two, full_two.astype(jnp.float32), precision=exact_mode)
        inverse_one = inverse_lower(diag_one)
        crossed = halving_scatter(
            jnp.dot(solved_two.T, trail, preferred_element_type=jnp.float32), "row", n_row
        )
        adj_two = adj_row_two - crossed - rest_two
        adj_next = adj_trail - jnp.dot(solved_two, full_two, preferred_element_type=jnp.float32)
        stacked = jnp.concatenate([adj_two[:, last:], adj_next[:, last:]], 0)
        solved_one = solve_panel(stacked, inverse_one, root_one)
        head_rows = solved_one[:band]
        tail_rows = solved_one[band:]
        partial_one = jnp.dot(
            head_rows.T, row_two[:, last:], preferred_element_type=jnp.float32
        ) + jnp.dot(tail_rows.T, trail[:, last:], preferred_element_type=jnp.float32)
        seed_one = jnp.tril(adj_diag_one - summed_block(partial_one, root_one))
        grad_diag_one = block_adjoint(diag_one, inverse_one, seed_one)
        mirror_one = own_rows(grad_diag_one + grad_diag_one.T)
        rest_one = jnp.dot(mirror_one, full_one.astype(jnp.float32), precision=exact_mode)
        head_update = jnp.dot(head_rows, full_one, preferred_element_type=jnp.float32)
        two_left = adj_two - head_update
        trail_left = adj_next - jnp.dot(tail_rows, full_one, preferred_element_type=jnp.float32)
        crossed_one = halving_scatter(
            jnp.dot(head_rows.T, row_two, preferred_element_type=jnp.float32)
            + jnp.dot(tail_rows.T, trail, preferred_element_type=jnp.float32),
            "row",
            n_row,
        )
        one_left = adj_row_one - crossed_one - rest_one
        trail_block = jnp.where(
            here_one,
            tail_rows.astype(jnp.float32),
            jnp.where(here_two, solved_two.astype(jnp.float32), trail_left[:, last:]),
        )
        grad_trail = jnp.concatenate([trail_left[:, :last], trail_block], 1).astype(jnp.bfloat16)
        zero_block = jnp.zeros((band, panel), jnp.float32)
        one_block = jnp.where(here_one | here_two, zero_block, one_left[:, last:])
        grad_row_one = jnp.concatenate([one_left[:, :last], one_block], 1)
        two_block = jnp.where(
            here_one, head_rows.astype(jnp.float32), jnp.where(here_two, zero_block, two_left[:, last:])
        )
        grad_row_two = jnp.concatenate([two_left[:, :last], two_block], 1)
        return (grad_trail, grad_row_one, grad_row_two, grad_diag_one, grad_diag_two)

    return per_device


def solution(mesh):
    in_specs = (
        P("row", "col"),
        P("row", "col"),
        P("row", "col"),
        P(),
        P(),
        P("row", "col"),
        P("row", "col"),
        P("row", "col"),
        P(),
        P(),
    )
    out_specs = (P("row", "col"), P("row", "col"), P("row", "col"), P(), P())
    return jax.shard_map(
        make_per_device(mesh.shape["row"], mesh.shape["col"]),
        mesh=mesh,
        in_specs=in_specs,
        out_specs=out_specs,
        check_vma=False,
    )
```

```python
import functools

import jax
import jax.numpy as jnp
from jax import lax
from jax.experimental import pallas as pl
from jax.experimental.pallas import tpu as pltpu
from jax.sharding import PartitionSpec as P

exact_mode = lax.Precision.HIGHEST


def spread_kernel(root, size, x_ref, y_ref, buf, recv_sem, send_sem):
    me = lax.axis_index("col")
    row = lax.axis_index("row")
    barrier = pltpu.get_barrier_semaphore()
    for step in range(1, size):
        pl.semaphore_signal(
            barrier,
            inc=1,
            device_id=(row, lax.rem(me + step, size)),
            device_id_type=pl.DeviceIdType.MESH,
        )
    pl.semaphore_wait(barrier, size - 1)
    rows = x_ref.shape[0] // size
    is_root = me == root

    def piece(p):
        return pl.ds(p * rows, rows)

    def copy(p, dest, src, phase):
        return pltpu.make_async_remote_copy(
            src_ref=src.at[piece(p)],
            dst_ref=buf.at[piece(p)],
            send_sem=send_sem.at[phase, dest],
            recv_sem=recv_sem.at[p],
            device_id=(row, dest),
            device_id_type=pl.DeviceIdType.MESH,
        )

    @pl.when(is_root)
    def _():
        for dest in range(size):
            if dest != root:
                copy(dest, dest, x_ref, 0).start()
        for dest in range(size):
            if dest != root:
                copy(root, dest, x_ref, 1).start()
        for dest in range(size):
            if dest != root:
                copy(dest, dest, x_ref, 0).wait_send()
                copy(root, dest, x_ref, 1).wait_send()
        y_ref[...] = x_ref[...]

    @pl.when(jnp.logical_not(is_root))
    def _():
        for own in range(size):
            if own == root:
                continue

            @pl.when(me == own)
            def _():
                copy(own, own, buf, 0).wait_recv()
                for dest in range(size):
                    if dest != root and dest != own:
                        copy(own, dest, buf, 1).start()
                for p in range(size):
                    if p != own:
                        copy(p, own, buf, 1).wait_recv()
                for dest in range(size):
                    if dest != root and dest != own:
                        copy(own, dest, buf, 1).wait_send()
        y_ref[...] = buf[...]


def panel_broadcast(value, size, root, call_id):
    return pl.pallas_call(
        functools.partial(spread_kernel, root, size),
        out_shape=jax.ShapeDtypeStruct(value.shape, value.dtype),
        in_specs=[pl.BlockSpec(memory_space=pltpu.VMEM)],
        out_specs=pl.BlockSpec(memory_space=pltpu.VMEM),
        scratch_shapes=[
            pltpu.VMEM(value.shape, value.dtype),
            pltpu.SemaphoreType.DMA((size,)),
            pltpu.SemaphoreType.DMA((2, size)),
        ],
        compiler_params=pltpu.CompilerParams(collective_id=call_id, has_side_effects=True),
    )(value)


def tree_broadcast(value, axis, size, root):
    here = lax.axis_index(axis) ^ root
    span = 1
    while span < size:
        radix = min(4, size // span)
        arrived = None
        for digit in range(1, radix):
            pairs = [(root ^ d, root ^ (d + digit * span)) for d in range(span)]
            part = lax.ppermute(value, axis, pairs)
            arrived = part if arrived is None else arrived + part
        take = (here >= span) & (here < radix * span)
        value = jnp.where(take, arrived, value)
        span *= radix
    return value


def butterfly_sum(value, axis, size):
    step = 1
    while step < size:
        pairs = [(i, i ^ step) for i in range(size)]
        value = value + lax.ppermute(value, axis, pairs)
        step *= 2
    return value


def halving_scatter(value, axis, size):
    here = lax.axis_index(axis)
    band = value.shape[0] // size
    blocks = value.reshape(size, band, value.shape[1])
    step = size // 2
    while step >= 1:
        halves = blocks.reshape(2, step, band, value.shape[1])
        high = ((here // step) % 2) == 1
        keep = jnp.where(high, halves[1], halves[0])
        send = jnp.where(high, halves[0], halves[1])
        pairs = [(i, i ^ step) for i in range(size)]
        blocks = keep + lax.ppermute(send, axis, pairs)
        step //= 2
    return blocks.reshape(band, value.shape[1])


def doubling_gather(value, axis, size):
    here = lax.axis_index(axis)
    step = 1
    while step < size:
        pairs = [(i, i ^ step) for i in range(size)]
        other = lax.ppermute(value, axis, pairs)
        high = ((here // step) % 2) == 1
        value = jnp.where(
            high,
            jnp.concatenate([other, value], 0),
            jnp.concatenate([value, other], 0),
        )
        step *= 2
    return value


def halved_lower(matrix):
    order = matrix.shape[0]
    keep = jnp.tril(jnp.ones((order, order), matrix.dtype)) - 0.5 * jnp.eye(
        order, dtype=matrix.dtype
    )
    return matrix * keep


def inverse_lower(block):
    ident = jnp.eye(block.shape[0], dtype=block.dtype)
    return lax.linalg.triangular_solve(block, ident, left_side=True, lower=True)


def block_adjoint(block, inverse, seed_adj):
    inner = halved_lower(jnp.dot(block.T, seed_adj, precision=exact_mode))
    middle = jnp.dot(inverse.T, inner, precision=exact_mode)
    return halved_lower(jnp.dot(middle, inverse, precision=exact_mode))


def make_per_device(n_row, n_col):
    def per_device(
        trail,
        row_one,
        row_two,
        diag_one,
        diag_two,
        adj_trail,
        adj_row_one,
        adj_row_two,
        adj_diag_one,
        adj_diag_two,
    ):
        panel = diag_one.shape[0]
        width = trail.shape[1]
        band = row_one.shape[0]
        last = width - panel
        col_here = lax.axis_index("col")
        row_start = lax.axis_index("row") * band
        root_one = n_col - 2
        root_two = n_col - 1
        here_one = col_here == root_one
        here_two = col_here == root_two
        full_one = doubling_gather(row_one, "row", n_row)
        full_two = doubling_gather(row_two, "row", n_row)

        def own_rows(matrix):
            return lax.dynamic_slice_in_dim(matrix, row_start, band, 0)

        def solve_panel(rows, inverse, root):
            local = jnp.dot(rows, inverse, precision=exact_mode).astype(jnp.bfloat16)
            head = local.shape[0] % (16 * n_col)
            tail = panel_broadcast(local[head:], n_col, root, n_col - 1 - root)
            if head == 0:
                return tail
            return jnp.concatenate([tree_broadcast(local[:head], "col", n_col, root), tail], 0)

        def summed_block(partial_value, root):
            rows_sum = butterfly_sum(partial_value, "row", n_row)
            return tree_broadcast(rows_sum, "col", n_col, root)

        inverse_two = inverse_lower(diag_two)
        solved_two = solve_panel(adj_trail[:, last:], inverse_two, root_two)
        partial_two = jnp.dot(solved_two.T, trail[:, last:], preferred_element_type=jnp.float32)
        seed_two = jnp.tril(adj_diag_two - summed_block(partial_two, root_two))
        grad_diag_two = block_adjoint(diag_two, inverse_two, seed_two)
        mirror_two = own_rows(grad_diag_two + grad_diag_two.T)
        rest_two = jnp.dot(mirror_two, full_two.astype(jnp.float32), precision=exact_mode)
        inverse_one = inverse_lower(diag_one)
        crossed = halving_scatter(
            jnp.dot(solved_two.T, trail, preferred_element_type=jnp.float32), "row", n_row
        )
        adj_two = adj_row_two - crossed - rest_two
        adj_next = adj_trail - jnp.dot(solved_two, full_two, preferred_element_type=jnp.float32)
        stacked = jnp.concatenate([adj_two[:, last:], adj_next[:, last:]], 0)
        solved_one = solve_panel(stacked, inverse_one, root_one)
        head_rows = solved_one[:band]
        tail_rows = solved_one[band:]
        partial_one = jnp.dot(
            head_rows.T, row_two[:, last:], preferred_element_type=jnp.float32
        ) + jnp.dot(tail_rows.T, trail[:, last:], preferred_element_type=jnp.float32)
        seed_one = jnp.tril(adj_diag_one - summed_block(partial_one, root_one))
        grad_diag_one = block_adjoint(diag_one, inverse_one, seed_one)
        mirror_one = own_rows(grad_diag_one + grad_diag_one.T)
        rest_one = jnp.dot(mirror_one, full_one.astype(jnp.float32), precision=exact_mode)
        head_update = jnp.dot(head_rows, full_one, preferred_element_type=jnp.float32)
        two_left = adj_two - head_update
        trail_left = adj_next - jnp.dot(tail_rows, full_one, preferred_element_type=jnp.float32)
        crossed_one = halving_scatter(
            jnp.dot(head_rows.T, row_two, preferred_element_type=jnp.float32)
            + jnp.dot(tail_rows.T, trail, preferred_element_type=jnp.float32),
            "row",
            n_row,
        )
        one_left = adj_row_one - crossed_one - rest_one
        trail_block = jnp.where(
            here_one,
            tail_rows.astype(jnp.float32),
            jnp.where(here_two, solved_two.astype(jnp.float32), trail_left[:, last:]),
        )
        grad_trail = jnp.concatenate([trail_left[:, :last], trail_block], 1).astype(jnp.bfloat16)
        zero_block = jnp.zeros((band, panel), jnp.float32)
        one_block = jnp.where(here_one | here_two, zero_block, one_left[:, last:])
        grad_row_one = jnp.concatenate([one_left[:, :last], one_block], 1)
        two_block = jnp.where(
            here_one, head_rows.astype(jnp.float32), jnp.where(here_two, zero_block, two_left[:, last:])
        )
        grad_row_two = jnp.concatenate([two_left[:, :last], two_block], 1)
        return (grad_trail, grad_row_one, grad_row_two, grad_diag_one, grad_diag_two)

    return per_device


def solution(mesh):
    in_specs = (
        P("row", "col"),
        P("row", "col"),
        P("row", "col"),
        P(),
        P(),
        P("row", "col"),
        P("row", "col"),
        P("row", "col"),
        P(),
        P(),
    )
    out_specs = (P("row", "col"), P("row", "col"), P("row", "col"), P(), P())
    return jax.shard_map(
        make_per_device(mesh.shape["row"], mesh.shape["col"]),
        mesh=mesh,
        in_specs=in_specs,
        out_specs=out_specs,
        check_vma=False,
    )
```

```python
import functools

import jax
import jax.numpy as jnp
from jax import lax
from jax.experimental import pallas as pl
from jax.experimental.pallas import tpu as pltpu
from jax.sharding import PartitionSpec as P

exact_mode = lax.Precision.HIGHEST


def spread_kernel(root, size, x_ref, y_ref, buf, recv_sem, send_sem):
    me = lax.axis_index("col")
    row = lax.axis_index("row")
    barrier = pltpu.get_barrier_semaphore()
    for step in range(1, size):
        pl.semaphore_signal(
            barrier,
            inc=1,
            device_id=(row, lax.rem(me + step, size)),
            device_id_type=pl.DeviceIdType.MESH,
        )
    pl.semaphore_wait(barrier, size - 1)
    rows = x_ref.shape[0] // size
    is_root = me == root

    def piece(p):
        return pl.ds(p * rows, rows)

    def copy(p, dest, src, phase):
        return pltpu.make_async_remote_copy(
            src_ref=src.at[piece(p)],
            dst_ref=buf.at[piece(p)],
            send_sem=send_sem.at[phase, dest],
            recv_sem=recv_sem.at[p],
            device_id=(row, dest),
            device_id_type=pl.DeviceIdType.MESH,
        )

    @pl.when(is_root)
    def _():
        for dest in range(size):
            if dest != root:
                copy(dest, dest, x_ref, 0).start()
        for dest in range(size):
            if dest != root:
                copy(root, dest, x_ref, 1).start()
        for dest in range(size):
            if dest != root:
                copy(dest, dest, x_ref, 0).wait_send()
                copy(root, dest, x_ref, 1).wait_send()
        y_ref[...] = x_ref[...]

    @pl.when(jnp.logical_not(is_root))
    def _():
        for own in range(size):
            if own == root:
                continue

            @pl.when(me == own)
            def _():
                copy(own, own, buf, 0).wait_recv()
                for dest in range(size):
                    if dest != root and dest != own:
                        copy(own, dest, buf, 1).start()
                for p in range(size):
                    if p != own:
                        copy(p, own, buf, 1).wait_recv()
                for dest in range(size):
                    if dest != root and dest != own:
                        copy(own, dest, buf, 1).wait_send()
        y_ref[...] = buf[...]


def panel_broadcast(value, size, root, call_id):
    return pl.pallas_call(
        functools.partial(spread_kernel, root, size),
        out_shape=jax.ShapeDtypeStruct(value.shape, value.dtype),
        in_specs=[pl.BlockSpec(memory_space=pltpu.VMEM)],
        out_specs=pl.BlockSpec(memory_space=pltpu.VMEM),
        scratch_shapes=[
            pltpu.VMEM(value.shape, value.dtype),
            pltpu.SemaphoreType.DMA((size,)),
            pltpu.SemaphoreType.DMA((2, size)),
        ],
        compiler_params=pltpu.CompilerParams(collective_id=call_id, has_side_effects=True),
    )(value)


def tree_broadcast(value, axis, size, root):
    here = lax.axis_index(axis) ^ root
    span = 1
    while span < size:
        radix = min(4, size // span)
        arrived = None
        for digit in range(1, radix):
            pairs = [(root ^ d, root ^ (d + digit * span)) for d in range(span)]
            part = lax.ppermute(value, axis, pairs)
            arrived = part if arrived is None else arrived + part
        take = (here >= span) & (here < radix * span)
        value = jnp.where(take, arrived, value)
        span *= radix
    return value


def butterfly_sum(value, axis, size):
    step = 1
    while step < size:
        pairs = [(i, i ^ step) for i in range(size)]
        value = value + lax.ppermute(value, axis, pairs)
        step *= 2
    return value


def halving_scatter(value, axis, size):
    here = lax.axis_index(axis)
    band = value.shape[0] // size
    blocks = value.reshape(size, band, value.shape[1])
    step = size // 2
    while step >= 1:
        halves = blocks.reshape(2, step, band, value.shape[1])
        high = ((here // step) % 2) == 1
        keep = jnp.where(high, halves[1], halves[0])
        send = jnp.where(high, halves[0], halves[1])
        pairs = [(i, i ^ step) for i in range(size)]
        blocks = keep + lax.ppermute(send, axis, pairs)
        step //= 2
    return blocks.reshape(band, value.shape[1])


def doubling_gather(value, axis, size):
    here = lax.axis_index(axis)
    step = 1
    while step < size:
        pairs = [(i, i ^ step) for i in range(size)]
        other = lax.ppermute(value, axis, pairs)
        high = ((here // step) % 2) == 1
        value = jnp.where(
            high,
            jnp.concatenate([other, value], 0),
            jnp.concatenate([value, other], 0),
        )
        step *= 2
    return value


def halved_lower(matrix):
    order = matrix.shape[0]
    keep = jnp.tril(jnp.ones((order, order), matrix.dtype)) - 0.5 * jnp.eye(
        order, dtype=matrix.dtype
    )
    return matrix * keep


def inverse_lower(block):
    ident = jnp.eye(block.shape[0], dtype=block.dtype)
    return lax.linalg.triangular_solve(block, ident, left_side=True, lower=True)


def block_adjoint(block, inverse, seed_adj):
    inner = halved_lower(jnp.dot(block.T, seed_adj, precision=exact_mode))
    middle = jnp.dot(inverse.T, inner, precision=exact_mode)
    return halved_lower(jnp.dot(middle, inverse, precision=exact_mode))


def make_per_device(n_row, n_col):
    def per_device(
        trail,
        row_one,
        row_two,
        diag_one,
        diag_two,
        adj_trail,
        adj_row_one,
        adj_row_two,
        adj_diag_one,
        adj_diag_two,
    ):
        panel = diag_one.shape[0]
        width = trail.shape[1]
        band = row_one.shape[0]
        last = width - panel
        col_here = lax.axis_index("col")
        row_start = lax.axis_index("row") * band
        root_one = n_col - 2
        root_two = n_col - 1
        here_one = col_here == root_one
        here_two = col_here == root_two
        full_one = doubling_gather(row_one, "row", n_row)
        full_two = doubling_gather(row_two, "row", n_row)

        def own_rows(matrix):
            return lax.dynamic_slice_in_dim(matrix, row_start, band, 0)

        def solve_panel(rows, inverse, root):
            local = jnp.dot(rows, inverse, precision=exact_mode).astype(jnp.bfloat16)
            head = local.shape[0] % (16 * n_col)
            tail = panel_broadcast(local[head:], n_col, root, n_col - 1 - root)
            if head == 0:
                return tail
            return jnp.concatenate([tree_broadcast(local[:head], "col", n_col, root), tail], 0)

        def summed_block(partial_value, root):
            rows_sum = butterfly_sum(partial_value, "row", n_row)
            return tree_broadcast(rows_sum, "col", n_col, root)

        inverse_two = inverse_lower(diag_two)
        solved_two = solve_panel(adj_trail[:, last:], inverse_two, root_two)
        partial_two = jnp.dot(solved_two.T, trail[:, last:], preferred_element_type=jnp.float32)
        seed_two = jnp.tril(adj_diag_two - summed_block(partial_two, root_two))
        grad_diag_two = block_adjoint(diag_two, inverse_two, seed_two)
        mirror_two = own_rows(grad_diag_two + grad_diag_two.T)
        rest_two = jnp.dot(mirror_two, full_two.astype(jnp.float32), precision=exact_mode)
        inverse_one = inverse_lower(diag_one)
        crossed = halving_scatter(
            jnp.dot(solved_two.T, trail, preferred_element_type=jnp.float32), "row", n_row
        )
        adj_two = adj_row_two - crossed - rest_two
        next_panel = adj_trail[:, last:] - jnp.dot(
            solved_two, full_two[:, last:], preferred_element_type=jnp.float32
        )
        stacked = jnp.concatenate([adj_two[:, last:], next_panel], 0)
        solved_one = solve_panel(stacked, inverse_one, root_one)
        head_rows = solved_one[:band]
        tail_rows = solved_one[band:]
        partial_one = jnp.dot(
            head_rows.T, row_two[:, last:], preferred_element_type=jnp.float32
        ) + jnp.dot(tail_rows.T, trail[:, last:], preferred_element_type=jnp.float32)
        seed_one = jnp.tril(adj_diag_one - summed_block(partial_one, root_one))
        grad_diag_one = block_adjoint(diag_one, inverse_one, seed_one)
        mirror_one = own_rows(grad_diag_one + grad_diag_one.T)
        rest_one = jnp.dot(mirror_one, full_one.astype(jnp.float32), precision=exact_mode)
        head_update = jnp.dot(head_rows, full_one, preferred_element_type=jnp.float32)
        two_left = adj_two - head_update
        trail_left = adj_trail - jnp.dot(
            jnp.concatenate([solved_two, tail_rows], 1),
            jnp.concatenate([full_two, full_one], 0),
            preferred_element_type=jnp.float32,
        )
        crossed_one = halving_scatter(
            jnp.dot(head_rows.T, row_two, preferred_element_type=jnp.float32)
            + jnp.dot(tail_rows.T, trail, preferred_element_type=jnp.float32),
            "row",
            n_row,
        )
        one_left = adj_row_one - crossed_one - rest_one
        trail_block = jnp.where(
            here_one,
            tail_rows.astype(jnp.float32),
            jnp.where(here_two, solved_two.astype(jnp.float32), trail_left[:, last:]),
        )
        grad_trail = jnp.concatenate([trail_left[:, :last], trail_block], 1).astype(jnp.bfloat16)
        zero_block = jnp.zeros((band, panel), jnp.float32)
        one_block = jnp.where(here_one | here_two, zero_block, one_left[:, last:])
        grad_row_one = jnp.concatenate([one_left[:, :last], one_block], 1)
        two_block = jnp.where(
            here_one, head_rows.astype(jnp.float32), jnp.where(here_two, zero_block, two_left[:, last:])
        )
        grad_row_two = jnp.concatenate([two_left[:, :last], two_block], 1)
        return (grad_trail, grad_row_one, grad_row_two, grad_diag_one, grad_diag_two)

    return per_device


def solution(mesh):
    in_specs = (
        P("row", "col"),
        P("row", "col"),
        P("row", "col"),
        P(),
        P(),
        P("row", "col"),
        P("row", "col"),
        P("row", "col"),
        P(),
        P(),
    )
    out_specs = (P("row", "col"), P("row", "col"), P("row", "col"), P(), P())
    return jax.shard_map(
        make_per_device(mesh.shape["row"], mesh.shape["col"]),
        mesh=mesh,
        in_specs=in_specs,
        out_specs=out_specs,
        check_vma=False,
    )
```

```python
import functools

import jax
import jax.numpy as jnp
from jax import lax
from jax.experimental import pallas as pl
from jax.experimental.pallas import tpu as pltpu
from jax.sharding import PartitionSpec as P

exact_mode = lax.Precision.HIGHEST


def spread_kernel(root, size, x_ref, y_ref, buf, recv_sem, send_sem):
    me = lax.axis_index("col")
    row = lax.axis_index("row")
    barrier = pltpu.get_barrier_semaphore()
    for step in range(1, size):
        pl.semaphore_signal(
            barrier,
            inc=1,
            device_id=(row, lax.rem(me + step, size)),
            device_id_type=pl.DeviceIdType.MESH,
        )
    pl.semaphore_wait(barrier, size - 1)
    rows = x_ref.shape[0] // size
    is_root = me == root

    def piece(p):
        return pl.ds(p * rows, rows)

    def copy(p, dest, src, phase):
        return pltpu.make_async_remote_copy(
            src_ref=src.at[piece(p)],
            dst_ref=buf.at[piece(p)],
            send_sem=send_sem.at[phase, dest],
            recv_sem=recv_sem.at[p],
            device_id=(row, dest),
            device_id_type=pl.DeviceIdType.MESH,
        )

    @pl.when(is_root)
    def _():
        for dest in range(size):
            if dest != root:
                copy(dest, dest, x_ref, 0).start()
        for dest in range(size):
            if dest != root:
                copy(root, dest, x_ref, 1).start()
        for dest in range(size):
            if dest != root:
                copy(dest, dest, x_ref, 0).wait_send()
                copy(root, dest, x_ref, 1).wait_send()
        y_ref[...] = x_ref[...]

    @pl.when(jnp.logical_not(is_root))
    def _():
        for own in range(size):
            if own == root:
                continue

            @pl.when(me == own)
            def _():
                copy(own, own, buf, 0).wait_recv()
                for dest in range(size):
                    if dest != root and dest != own:
                        copy(own, dest, buf, 1).start()
                for p in range(size):
                    if p != own:
                        copy(p, own, buf, 1).wait_recv()
                for dest in range(size):
                    if dest != root and dest != own:
                        copy(own, dest, buf, 1).wait_send()
        y_ref[...] = buf[...]


def panel_broadcast(value, size, root, call_id):
    return pl.pallas_call(
        functools.partial(spread_kernel, root, size),
        out_shape=jax.ShapeDtypeStruct(value.shape, value.dtype),
        in_specs=[pl.BlockSpec(memory_space=pltpu.VMEM)],
        out_specs=pl.BlockSpec(memory_space=pltpu.VMEM),
        scratch_shapes=[
            pltpu.VMEM(value.shape, value.dtype),
            pltpu.SemaphoreType.DMA((size,)),
            pltpu.SemaphoreType.DMA((2, size)),
        ],
        compiler_params=pltpu.CompilerParams(collective_id=call_id, has_side_effects=True),
    )(value)


def tree_broadcast(value, axis, size, root):
    here = lax.axis_index(axis) ^ root
    span = 1
    while span < size:
        radix = min(4, size // span)
        arrived = None
        for digit in range(1, radix):
            pairs = [(root ^ d, root ^ (d + digit * span)) for d in range(span)]
            part = lax.ppermute(value, axis, pairs)
            arrived = part if arrived is None else arrived + part
        take = (here >= span) & (here < radix * span)
        value = jnp.where(take, arrived, value)
        span *= radix
    return value


def butterfly_sum(value, axis, size):
    step = 1
    while step < size:
        pairs = [(i, i ^ step) for i in range(size)]
        value = value + lax.ppermute(value, axis, pairs)
        step *= 2
    return value


def halving_scatter(value, axis, size):
    here = lax.axis_index(axis)
    band = value.shape[0] // size
    blocks = value.reshape(size, band, value.shape[1])
    step = size // 2
    while step >= 1:
        halves = blocks.reshape(2, step, band, value.shape[1])
        high = ((here // step) % 2) == 1
        keep = jnp.where(high, halves[1], halves[0])
        send = jnp.where(high, halves[0], halves[1])
        pairs = [(i, i ^ step) for i in range(size)]
        blocks = keep + lax.ppermute(send, axis, pairs)
        step //= 2
    return blocks.reshape(band, value.shape[1])


def doubling_gather(value, axis, size):
    here = lax.axis_index(axis)
    step = 1
    while step < size:
        pairs = [(i, i ^ step) for i in range(size)]
        other = lax.ppermute(value, axis, pairs)
        high = ((here // step) % 2) == 1
        value = jnp.where(
            high,
            jnp.concatenate([other, value], 0),
            jnp.concatenate([value, other], 0),
        )
        step *= 2
    return value


def halved_lower(matrix):
    order = matrix.shape[0]
    keep = jnp.tril(jnp.ones((order, order), matrix.dtype)) - 0.5 * jnp.eye(
        order, dtype=matrix.dtype
    )
    return matrix * keep


def inverse_lower(block):
    ident = jnp.eye(block.shape[0], dtype=block.dtype)
    return lax.linalg.triangular_solve(block, ident, left_side=True, lower=True)


def block_adjoint(block, inverse, seed_adj):
    inner = halved_lower(jnp.dot(block.T, seed_adj, precision=exact_mode))
    middle = jnp.dot(inverse.T, inner, precision=exact_mode)
    return halved_lower(jnp.dot(middle, inverse, precision=exact_mode))


def make_per_device(n_row, n_col):
    def per_device(
        trail,
        row_one,
        row_two,
        diag_one,
        diag_two,
        adj_trail,
        adj_row_one,
        adj_row_two,
        adj_diag_one,
        adj_diag_two,
    ):
        panel = diag_one.shape[0]
        width = trail.shape[1]
        band = row_one.shape[0]
        last = width - panel
        col_here = lax.axis_index("col")
        row_start = lax.axis_index("row") * band
        root_one = n_col - 2
        root_two = n_col - 1
        here_one = col_here == root_one
        here_two = col_here == root_two
        full_one = doubling_gather(row_one, "row", n_row)
        full_two = doubling_gather(row_two, "row", n_row)

        def own_rows(matrix):
            return lax.dynamic_slice_in_dim(matrix, row_start, band, 0)

        def solve_panel(rows, inverse, root):
            local = jnp.dot(rows, inverse, precision=exact_mode).astype(jnp.bfloat16)
            head = local.shape[0] % (16 * n_col)
            tail = panel_broadcast(local[head:], n_col, root, n_col - 1 - root)
            if head == 0:
                return tail
            return jnp.concatenate([tree_broadcast(local[:head], "col", n_col, root), tail], 0)

        def summed_block(partial_value, root):
            rows_sum = butterfly_sum(partial_value, "row", n_row)
            return tree_broadcast(rows_sum, "col", n_col, root)

        inverse_two = inverse_lower(diag_two)
        solved_two = solve_panel(adj_trail[:, last:], inverse_two, root_two)
        partial_two = jnp.dot(solved_two.T, trail[:, last:], preferred_element_type=jnp.float32)
        seed_two = jnp.tril(adj_diag_two - summed_block(partial_two, root_two))
        grad_diag_two = block_adjoint(diag_two, inverse_two, seed_two)
        mirror_two = own_rows(grad_diag_two + grad_diag_two.T)
        rest_two = jnp.dot(mirror_two, full_two.astype(jnp.float32), precision=exact_mode)
        inverse_one = inverse_lower(diag_one)
        crossed = halving_scatter(
            jnp.dot(solved_two.T, trail, preferred_element_type=jnp.float32), "row", n_row
        )
        adj_two = adj_row_two - crossed - rest_two
        next_panel = adj_trail[:, last:] - jnp.dot(
            solved_two, full_two[:, last:], preferred_element_type=jnp.float32
        )
        stacked = jnp.concatenate([adj_two[:, last:], next_panel], 0)
        solved_one = solve_panel(stacked, inverse_one, root_one)
        head_rows = solved_one[:band]
        tail_rows = solved_one[band:]
        partial_one = jnp.dot(
            head_rows.T, row_two[:, last:], preferred_element_type=jnp.float32
        ) + jnp.dot(tail_rows.T, trail[:, last:], preferred_element_type=jnp.float32)
        rows_one = butterfly_sum(partial_one, "row", n_row)
        tail_late, rows_one = lax.optimization_barrier((tail_rows, rows_one))
        seed_one = jnp.tril(adj_diag_one - tree_broadcast(rows_one, "col", n_col, root_one))
        grad_diag_one = block_adjoint(diag_one, inverse_one, seed_one)
        mirror_one = own_rows(grad_diag_one + grad_diag_one.T)
        rest_one = jnp.dot(mirror_one, full_one.astype(jnp.float32), precision=exact_mode)
        head_update = jnp.dot(head_rows, full_one, preferred_element_type=jnp.float32)
        two_left = adj_two - head_update
        trail_left = adj_trail - jnp.dot(
            jnp.concatenate([solved_two, tail_late], 1),
            jnp.concatenate([full_two, full_one], 0),
            preferred_element_type=jnp.float32,
        )
        crossed_one = halving_scatter(
            jnp.dot(head_rows.T, row_two, preferred_element_type=jnp.float32)
            + jnp.dot(tail_rows.T, trail, preferred_element_type=jnp.float32),
            "row",
            n_row,
        )
        one_left = adj_row_one - crossed_one - rest_one
        trail_block = jnp.where(
            here_one,
            tail_rows.astype(jnp.float32),
            jnp.where(here_two, solved_two.astype(jnp.float32), trail_left[:, last:]),
        )
        grad_trail = jnp.concatenate([trail_left[:, :last], trail_block], 1).astype(jnp.bfloat16)
        zero_block = jnp.zeros((band, panel), jnp.float32)
        one_block = jnp.where(here_one | here_two, zero_block, one_left[:, last:])
        grad_row_one = jnp.concatenate([one_left[:, :last], one_block], 1)
        two_block = jnp.where(
            here_one, head_rows.astype(jnp.float32), jnp.where(here_two, zero_block, two_left[:, last:])
        )
        grad_row_two = jnp.concatenate([two_left[:, :last], two_block], 1)
        return (grad_trail, grad_row_one, grad_row_two, grad_diag_one, grad_diag_two)

    return per_device


def solution(mesh):
    in_specs = (
        P("row", "col"),
        P("row", "col"),
        P("row", "col"),
        P(),
        P(),
        P("row", "col"),
        P("row", "col"),
        P("row", "col"),
        P(),
        P(),
    )
    out_specs = (P("row", "col"), P("row", "col"), P("row", "col"), P(), P())
    return jax.shard_map(
        make_per_device(mesh.shape["row"], mesh.shape["col"]),
        mesh=mesh,
        in_specs=in_specs,
        out_specs=out_specs,
        check_vma=False,
    )
```

```python
import functools

import jax
import jax.numpy as jnp
from jax import lax
from jax.experimental import pallas as pl
from jax.experimental.pallas import tpu as pltpu
from jax.sharding import PartitionSpec as P

exact_mode = lax.Precision.HIGHEST


def spread_kernel(root, size, x_ref, y_ref, buf, recv_sem, send_sem):
    me = lax.axis_index("col")
    row = lax.axis_index("row")
    barrier = pltpu.get_barrier_semaphore()
    for step in range(1, size):
        pl.semaphore_signal(
            barrier,
            inc=1,
            device_id=(row, lax.rem(me + step, size)),
            device_id_type=pl.DeviceIdType.MESH,
        )
    pl.semaphore_wait(barrier, size - 1)
    rows = x_ref.shape[0] // size
    is_root = me == root

    def piece(p):
        return pl.ds(p * rows, rows)

    def copy(p, dest, src, phase):
        return pltpu.make_async_remote_copy(
            src_ref=src.at[piece(p)],
            dst_ref=buf.at[piece(p)],
            send_sem=send_sem.at[phase, dest],
            recv_sem=recv_sem.at[p],
            device_id=(row, dest),
            device_id_type=pl.DeviceIdType.MESH,
        )

    @pl.when(is_root)
    def _():
        for dest in range(size):
            if dest != root:
                copy(dest, dest, x_ref, 0).start()
        for dest in range(size):
            if dest != root:
                copy(root, dest, x_ref, 1).start()
        for dest in range(size):
            if dest != root:
                copy(dest, dest, x_ref, 0).wait_send()
                copy(root, dest, x_ref, 1).wait_send()
        y_ref[...] = x_ref[...]

    @pl.when(jnp.logical_not(is_root))
    def _():
        for own in range(size):
            if own == root:
                continue

            @pl.when(me == own)
            def _():
                copy(own, own, buf, 0).wait_recv()
                for dest in range(size):
                    if dest != root and dest != own:
                        copy(own, dest, buf, 1).start()
                for p in range(size):
                    if p != own:
                        copy(p, own, buf, 1).wait_recv()
                for dest in range(size):
                    if dest != root and dest != own:
                        copy(own, dest, buf, 1).wait_send()
        y_ref[...] = buf[...]


def panel_broadcast(value, size, root, call_id):
    return pl.pallas_call(
        functools.partial(spread_kernel, root, size),
        out_shape=jax.ShapeDtypeStruct(value.shape, value.dtype),
        in_specs=[pl.BlockSpec(memory_space=pltpu.VMEM)],
        out_specs=pl.BlockSpec(memory_space=pltpu.VMEM),
        scratch_shapes=[
            pltpu.VMEM(value.shape, value.dtype),
            pltpu.SemaphoreType.DMA((size,)),
            pltpu.SemaphoreType.DMA((2, size)),
        ],
        compiler_params=pltpu.CompilerParams(collective_id=call_id, has_side_effects=True),
    )(value)


def tree_broadcast(value, axis, size, root):
    here = lax.axis_index(axis) ^ root
    span = 1
    while span < size:
        radix = min(4, size // span)
        arrived = None
        for digit in range(1, radix):
            pairs = [(root ^ d, root ^ (d + digit * span)) for d in range(span)]
            part = lax.ppermute(value, axis, pairs)
            arrived = part if arrived is None else arrived + part
        take = (here >= span) & (here < radix * span)
        value = jnp.where(take, arrived, value)
        span *= radix
    return value


def butterfly_sum(value, axis, size):
    step = 1
    while step < size:
        pairs = [(i, i ^ step) for i in range(size)]
        value = value + lax.ppermute(value, axis, pairs)
        step *= 2
    return value


def halving_scatter(value, axis, size):
    here = lax.axis_index(axis)
    band = value.shape[0] // size
    blocks = value.reshape(size, band, value.shape[1])
    step = size // 2
    while step >= 1:
        halves = blocks.reshape(2, step, band, value.shape[1])
        high = ((here // step) % 2) == 1
        keep = jnp.where(high, halves[1], halves[0])
        send = jnp.where(high, halves[0], halves[1])
        pairs = [(i, i ^ step) for i in range(size)]
        blocks = keep + lax.ppermute(send, axis, pairs)
        step //= 2
    return blocks.reshape(band, value.shape[1])


def doubling_gather(value, axis, size):
    here = lax.axis_index(axis)
    step = 1
    while step < size:
        pairs = [(i, i ^ step) for i in range(size)]
        other = lax.ppermute(value, axis, pairs)
        high = ((here // step) % 2) == 1
        value = jnp.where(
            high,
            jnp.concatenate([other, value], 0),
            jnp.concatenate([value, other], 0),
        )
        step *= 2
    return value


def halved_lower(matrix):
    order = matrix.shape[0]
    keep = jnp.tril(jnp.ones((order, order), matrix.dtype)) - 0.5 * jnp.eye(
        order, dtype=matrix.dtype
    )
    return matrix * keep


def inverse_lower(block):
    ident = jnp.eye(block.shape[0], dtype=block.dtype)
    return lax.linalg.triangular_solve(block, ident, left_side=True, lower=True)


def block_adjoint(block, inverse, seed_adj):
    inner = halved_lower(jnp.dot(block.T, seed_adj, precision=exact_mode))
    middle = jnp.dot(inverse.T, inner, precision=exact_mode)
    return halved_lower(jnp.dot(middle, inverse, precision=exact_mode))


def make_per_device(n_row, n_col):
    def per_device(
        trail,
        row_one,
        row_two,
        diag_one,
        diag_two,
        adj_trail,
        adj_row_one,
        adj_row_two,
        adj_diag_one,
        adj_diag_two,
    ):
        panel = diag_one.shape[0]
        width = trail.shape[1]
        band = row_one.shape[0]
        last = width - panel
        col_here = lax.axis_index("col")
        row_start = lax.axis_index("row") * band
        root_one = n_col - 2
        root_two = n_col - 1
        here_one = col_here == root_one
        here_two = col_here == root_two
        full_one = doubling_gather(row_one, "row", n_row)
        full_two = doubling_gather(row_two, "row", n_row)

        def own_rows(matrix):
            return lax.dynamic_slice_in_dim(matrix, row_start, band, 0)

        def solve_panel(rows, inverse, root):
            local = jnp.dot(rows, inverse, precision=exact_mode).astype(jnp.bfloat16)
            head = local.shape[0] % (16 * n_col)
            tail = panel_broadcast(local[head:], n_col, root, n_col - 1 - root)
            if head == 0:
                return tail
            return jnp.concatenate([tree_broadcast(local[:head], "col", n_col, root), tail], 0)

        def summed_block(partial_value, root):
            rows_sum = butterfly_sum(partial_value, "row", n_row)
            return tree_broadcast(rows_sum, "col", n_col, root)

        inverse_two = inverse_lower(diag_two)
        solved_two = solve_panel(adj_trail[:, last:], inverse_two, root_two)
        partial_two = jnp.dot(solved_two.T, trail[:, last:], preferred_element_type=jnp.float32)
        seed_two = jnp.tril(adj_diag_two - summed_block(partial_two, root_two))
        grad_diag_two = block_adjoint(diag_two, inverse_two, seed_two)
        mirror_two = own_rows(grad_diag_two + grad_diag_two.T)
        rest_two = jnp.dot(mirror_two, full_two.astype(jnp.float32), precision=exact_mode)
        inverse_one = inverse_lower(diag_one)
        crossed = halving_scatter(
            jnp.dot(solved_two.T, trail, preferred_element_type=jnp.float32), "row", n_row
        )
        adj_two = adj_row_two - crossed - rest_two
        next_panel = adj_trail[:, last:] - jnp.dot(
            solved_two, full_two[:, last:], preferred_element_type=jnp.float32
        )
        stacked = jnp.concatenate([adj_two[:, last:], next_panel], 0)
        solved_one = solve_panel(stacked, inverse_one, root_one)
        head_rows = solved_one[:band]
        tail_rows = solved_one[band:]
        partial_one = jnp.dot(
            head_rows.T, row_two[:, last:], preferred_element_type=jnp.float32
        ) + jnp.dot(tail_rows.T, trail[:, last:], preferred_element_type=jnp.float32)
        rows_one = butterfly_sum(partial_one, "row", n_row)
        tail_late, rows_one = lax.optimization_barrier((tail_rows, rows_one))
        seed_one = jnp.tril(adj_diag_one - tree_broadcast(rows_one, "col", n_col, root_one))
        grad_diag_one = block_adjoint(diag_one, inverse_one, seed_one)
        mirror_one = own_rows(grad_diag_one + grad_diag_one.T)
        rest_one = jnp.dot(mirror_one, full_one.astype(jnp.float32), precision=exact_mode)
        head_update = jnp.dot(head_rows, full_one, preferred_element_type=jnp.float32)
        two_left = adj_two - head_update
        trail_left = adj_trail - jnp.dot(
            jnp.concatenate([solved_two, tail_late], 1),
            jnp.concatenate([full_two, full_one], 0),
            preferred_element_type=jnp.float32,
        )
        crossed_one = halving_scatter(
            jnp.dot(head_rows.T, row_two, preferred_element_type=jnp.float32)
            + jnp.dot(tail_late.T, trail, preferred_element_type=jnp.float32),
            "row",
            n_row,
        )
        one_left = adj_row_one - crossed_one - rest_one
        trail_block = jnp.where(
            here_one,
            tail_rows.astype(jnp.float32),
            jnp.where(here_two, solved_two.astype(jnp.float32), trail_left[:, last:]),
        )
        grad_trail = jnp.concatenate([trail_left[:, :last], trail_block], 1).astype(jnp.bfloat16)
        zero_block = jnp.zeros((band, panel), jnp.float32)
        one_block = jnp.where(here_one | here_two, zero_block, one_left[:, last:])
        grad_row_one = jnp.concatenate([one_left[:, :last], one_block], 1)
        two_block = jnp.where(
            here_one, head_rows.astype(jnp.float32), jnp.where(here_two, zero_block, two_left[:, last:])
        )
        grad_row_two = jnp.concatenate([two_left[:, :last], two_block], 1)
        return (grad_trail, grad_row_one, grad_row_two, grad_diag_one, grad_diag_two)

    return per_device


def solution(mesh):
    in_specs = (
        P("row", "col"),
        P("row", "col"),
        P("row", "col"),
        P(),
        P(),
        P("row", "col"),
        P("row", "col"),
        P("row", "col"),
        P(),
        P(),
    )
    out_specs = (P("row", "col"), P("row", "col"), P("row", "col"), P(), P())
    return jax.shard_map(
        make_per_device(mesh.shape["row"], mesh.shape["col"]),
        mesh=mesh,
        in_specs=in_specs,
        out_specs=out_specs,
        check_vma=False,
    )
```

```python
import functools

import jax
import jax.numpy as jnp
from jax import lax
from jax.experimental import pallas as pl
from jax.experimental.pallas import tpu as pltpu
from jax.sharding import PartitionSpec as P

exact_mode = lax.Precision.HIGHEST


def spread_kernel(root, size, x_ref, y_ref, buf, recv_sem, send_sem):
    me = lax.axis_index("col")
    row = lax.axis_index("row")
    barrier = pltpu.get_barrier_semaphore()
    for step in range(1, size):
        pl.semaphore_signal(
            barrier,
            inc=1,
            device_id=(row, lax.rem(me + step, size)),
            device_id_type=pl.DeviceIdType.MESH,
        )
    pl.semaphore_wait(barrier, size - 1)
    rows = x_ref.shape[0] // size
    is_root = me == root

    def piece(p):
        return pl.ds(p * rows, rows)

    def copy(p, dest, src, phase):
        return pltpu.make_async_remote_copy(
            src_ref=src.at[piece(p)],
            dst_ref=buf.at[piece(p)],
            send_sem=send_sem.at[phase, dest],
            recv_sem=recv_sem.at[p],
            device_id=(row, dest),
            device_id_type=pl.DeviceIdType.MESH,
        )

    @pl.when(is_root)
    def _():
        for dest in range(size):
            if dest != root:
                copy(dest, dest, x_ref, 0).start()
        for dest in range(size):
            if dest != root:
                copy(root, dest, x_ref, 1).start()
        for dest in range(size):
            if dest != root:
                copy(dest, dest, x_ref, 0).wait_send()
                copy(root, dest, x_ref, 1).wait_send()
        y_ref[...] = x_ref[...]

    @pl.when(jnp.logical_not(is_root))
    def _():
        for own in range(size):
            if own == root:
                continue

            @pl.when(me == own)
            def _():
                copy(own, own, buf, 0).wait_recv()
                for dest in range(size):
                    if dest != root and dest != own:
                        copy(own, dest, buf, 1).start()
                for p in range(size):
                    if p != own:
                        copy(p, own, buf, 1).wait_recv()
                for dest in range(size):
                    if dest != root and dest != own:
                        copy(own, dest, buf, 1).wait_send()
        y_ref[...] = buf[...]


def panel_broadcast(value, size, root, call_id):
    return pl.pallas_call(
        functools.partial(spread_kernel, root, size),
        out_shape=jax.ShapeDtypeStruct(value.shape, value.dtype),
        in_specs=[pl.BlockSpec(memory_space=pltpu.VMEM)],
        out_specs=pl.BlockSpec(memory_space=pltpu.VMEM),
        scratch_shapes=[
            pltpu.VMEM(value.shape, value.dtype),
            pltpu.SemaphoreType.DMA((size,)),
            pltpu.SemaphoreType.DMA((2, size)),
        ],
        compiler_params=pltpu.CompilerParams(collective_id=call_id, has_side_effects=True),
    )(value)


def tree_broadcast(value, axis, size, root):
    here = lax.axis_index(axis) ^ root
    span = 1
    while span < size:
        radix = min(4, size // span)
        arrived = None
        for digit in range(1, radix):
            pairs = [(root ^ d, root ^ (d + digit * span)) for d in range(span)]
            part = lax.ppermute(value, axis, pairs)
            arrived = part if arrived is None else arrived + part
        take = (here >= span) & (here < radix * span)
        value = jnp.where(take, arrived, value)
        span *= radix
    return value


def butterfly_sum(value, axis, size):
    step = 1
    while step < size:
        pairs = [(i, i ^ step) for i in range(size)]
        value = value + lax.ppermute(value, axis, pairs)
        step *= 2
    return value


def halving_scatter(value, axis, size):
    here = lax.axis_index(axis)
    band = value.shape[0] // size
    blocks = value.reshape(size, band, value.shape[1])
    step = size // 2
    while step >= 1:
        halves = blocks.reshape(2, step, band, value.shape[1])
        high = ((here // step) % 2) == 1
        keep = jnp.where(high, halves[1], halves[0])
        send = jnp.where(high, halves[0], halves[1])
        pairs = [(i, i ^ step) for i in range(size)]
        blocks = keep + lax.ppermute(send, axis, pairs)
        step //= 2
    return blocks.reshape(band, value.shape[1])


def doubling_gather(value, axis, size):
    here = lax.axis_index(axis)
    step = 1
    while step < size:
        pairs = [(i, i ^ step) for i in range(size)]
        other = lax.ppermute(value, axis, pairs)
        high = ((here // step) % 2) == 1
        value = jnp.where(
            high,
            jnp.concatenate([other, value], 0),
            jnp.concatenate([value, other], 0),
        )
        step *= 2
    return value


def halved_lower(matrix):
    order = matrix.shape[0]
    keep = jnp.tril(jnp.ones((order, order), matrix.dtype)) - 0.5 * jnp.eye(
        order, dtype=matrix.dtype
    )
    return matrix * keep


def inverse_lower(block):
    ident = jnp.eye(block.shape[0], dtype=block.dtype)
    return lax.linalg.triangular_solve(block, ident, left_side=True, lower=True)


def block_adjoint(block, inverse, seed_adj):
    inner = halved_lower(jnp.dot(block.T, seed_adj, precision=exact_mode))
    middle = jnp.dot(inverse.T, inner, precision=exact_mode)
    return halved_lower(jnp.dot(middle, inverse, precision=exact_mode))


def make_per_device(n_row, n_col):
    def per_device(
        trail,
        row_one,
        row_two,
        diag_one,
        diag_two,
        adj_trail,
        adj_row_one,
        adj_row_two,
        adj_diag_one,
        adj_diag_two,
    ):
        panel = diag_one.shape[0]
        width = trail.shape[1]
        band = row_one.shape[0]
        last = width - panel
        col_here = lax.axis_index("col")
        row_start = lax.axis_index("row") * band
        root_one = n_col - 2
        root_two = n_col - 1
        here_one = col_here == root_one
        here_two = col_here == root_two
        full_one = doubling_gather(row_one, "row", n_row)
        full_two = doubling_gather(row_two, "row", n_row)

        def own_rows(matrix):
            return lax.dynamic_slice_in_dim(matrix, row_start, band, 0)

        def solve_panel(rows, inverse, root):
            local = jnp.dot(rows, inverse, precision=lax.Precision.HIGH).astype(jnp.bfloat16)
            head = local.shape[0] % (16 * n_col)
            tail = panel_broadcast(local[head:], n_col, root, n_col - 1 - root)
            if head == 0:
                return tail
            return jnp.concatenate([tree_broadcast(local[:head], "col", n_col, root), tail], 0)

        def summed_block(partial_value, root):
            rows_sum = butterfly_sum(partial_value, "row", n_row)
            return tree_broadcast(rows_sum, "col", n_col, root)

        inverse_two = inverse_lower(diag_two)
        solved_two = solve_panel(adj_trail[:, last:], inverse_two, root_two)
        partial_two = jnp.dot(solved_two.T, trail[:, last:], preferred_element_type=jnp.float32)
        seed_two = jnp.tril(adj_diag_two - summed_block(partial_two, root_two))
        grad_diag_two = block_adjoint(diag_two, inverse_two, seed_two)
        mirror_two = own_rows(grad_diag_two + grad_diag_two.T)
        rest_two = jnp.dot(mirror_two, full_two.astype(jnp.float32), precision=exact_mode)
        inverse_one = inverse_lower(diag_one)
        crossed = halving_scatter(
            jnp.dot(solved_two.T, trail, preferred_element_type=jnp.float32), "row", n_row
        )
        adj_two = adj_row_two - crossed - rest_two
        next_panel = adj_trail[:, last:] - jnp.dot(
            solved_two, full_two[:, last:], preferred_element_type=jnp.float32
        )
        stacked = jnp.concatenate([adj_two[:, last:], next_panel], 0)
        solved_one = solve_panel(stacked, inverse_one, root_one)
        head_rows = solved_one[:band]
        tail_rows = solved_one[band:]
        partial_one = jnp.dot(
            head_rows.T, row_two[:, last:], preferred_element_type=jnp.float32
        ) + jnp.dot(tail_rows.T, trail[:, last:], preferred_element_type=jnp.float32)
        rows_one = butterfly_sum(partial_one, "row", n_row)
        tail_late, rows_one = lax.optimization_barrier((tail_rows, rows_one))
        seed_one = jnp.tril(adj_diag_one - tree_broadcast(rows_one, "col", n_col, root_one))
        grad_diag_one = block_adjoint(diag_one, inverse_one, seed_one)
        mirror_one = own_rows(grad_diag_one + grad_diag_one.T)
        rest_one = jnp.dot(mirror_one, full_one.astype(jnp.float32), precision=exact_mode)
        head_update = jnp.dot(head_rows, full_one, preferred_element_type=jnp.float32)
        two_left = adj_two - head_update
        trail_left = adj_trail - jnp.dot(
            jnp.concatenate([solved_two, tail_late], 1),
            jnp.concatenate([full_two, full_one], 0),
            preferred_element_type=jnp.float32,
        )
        crossed_one = halving_scatter(
            jnp.dot(head_rows.T, row_two, preferred_element_type=jnp.float32)
            + jnp.dot(tail_rows.T, trail, preferred_element_type=jnp.float32),
            "row",
            n_row,
        )
        one_left = adj_row_one - crossed_one - rest_one
        trail_block = jnp.where(
            here_one,
            tail_rows.astype(jnp.float32),
            jnp.where(here_two, solved_two.astype(jnp.float32), trail_left[:, last:]),
        )
        grad_trail = jnp.concatenate([trail_left[:, :last], trail_block], 1).astype(jnp.bfloat16)
        zero_block = jnp.zeros((band, panel), jnp.float32)
        one_block = jnp.where(here_one | here_two, zero_block, one_left[:, last:])
        grad_row_one = jnp.concatenate([one_left[:, :last], one_block], 1)
        two_block = jnp.where(
            here_one, head_rows.astype(jnp.float32), jnp.where(here_two, zero_block, two_left[:, last:])
        )
        grad_row_two = jnp.concatenate([two_left[:, :last], two_block], 1)
        return (grad_trail, grad_row_one, grad_row_two, grad_diag_one, grad_diag_two)

    return per_device


def solution(mesh):
    in_specs = (
        P("row", "col"),
        P("row", "col"),
        P("row", "col"),
        P(),
        P(),
        P("row", "col"),
        P("row", "col"),
        P("row", "col"),
        P(),
        P(),
    )
    out_specs = (P("row", "col"), P("row", "col"), P("row", "col"), P(), P())
    return jax.shard_map(
        make_per_device(mesh.shape["row"], mesh.shape["col"]),
        mesh=mesh,
        in_specs=in_specs,
        out_specs=out_specs,
        check_vma=False,
    )
```

```python
import functools

import jax
import jax.numpy as jnp
from jax import lax
from jax.experimental import pallas as pl
from jax.experimental.pallas import tpu as pltpu
from jax.sharding import PartitionSpec as P

exact_mode = lax.Precision.HIGHEST


def spread_kernel(root, size, x_ref, y_ref, buf, recv_sem, send_sem):
    me = lax.axis_index("col")
    row = lax.axis_index("row")
    barrier = pltpu.get_barrier_semaphore()
    for step in range(1, size):
        pl.semaphore_signal(
            barrier,
            inc=1,
            device_id=(row, lax.rem(me + step, size)),
            device_id_type=pl.DeviceIdType.MESH,
        )
    pl.semaphore_wait(barrier, size - 1)
    rows = x_ref.shape[0] // size
    is_root = me == root

    def piece(p):
        return pl.ds(p * rows, rows)

    def copy(p, dest, src, phase):
        return pltpu.make_async_remote_copy(
            src_ref=src.at[piece(p)],
            dst_ref=buf.at[piece(p)],
            send_sem=send_sem.at[phase, dest],
            recv_sem=recv_sem.at[p],
            device_id=(row, dest),
            device_id_type=pl.DeviceIdType.MESH,
        )

    @pl.when(is_root)
    def _():
        for dest in range(size):
            if dest != root:
                copy(dest, dest, x_ref, 0).start()
        for dest in range(size):
            if dest != root:
                copy(root, dest, x_ref, 1).start()
        for dest in range(size):
            if dest != root:
                copy(dest, dest, x_ref, 0).wait_send()
                copy(root, dest, x_ref, 1).wait_send()
        y_ref[...] = x_ref[...]

    @pl.when(jnp.logical_not(is_root))
    def _():
        for own in range(size):
            if own == root:
                continue

            @pl.when(me == own)
            def _():
                copy(own, own, buf, 0).wait_recv()
                for dest in range(size):
                    if dest != root and dest != own:
                        copy(own, dest, buf, 1).start()
                for p in range(size):
                    if p != own:
                        copy(p, own, buf, 1).wait_recv()
                for dest in range(size):
                    if dest != root and dest != own:
                        copy(own, dest, buf, 1).wait_send()
        y_ref[...] = buf[...]


def panel_broadcast(value, size, root, call_id):
    return pl.pallas_call(
        functools.partial(spread_kernel, root, size),
        out_shape=jax.ShapeDtypeStruct(value.shape, value.dtype),
        in_specs=[pl.BlockSpec(memory_space=pltpu.VMEM)],
        out_specs=pl.BlockSpec(memory_space=pltpu.VMEM),
        scratch_shapes=[
            pltpu.VMEM(value.shape, value.dtype),
            pltpu.SemaphoreType.DMA((size,)),
            pltpu.SemaphoreType.DMA((2, size)),
        ],
        compiler_params=pltpu.CompilerParams(collective_id=call_id, has_side_effects=True),
    )(value)


def tree_broadcast(value, axis, size, root):
    here = lax.axis_index(axis) ^ root
    span = 1
    while span < size:
        radix = min(4, size // span)
        arrived = None
        for digit in range(1, radix):
            pairs = [(root ^ d, root ^ (d + digit * span)) for d in range(span)]
            part = lax.ppermute(value, axis, pairs)
            arrived = part if arrived is None else arrived + part
        take = (here >= span) & (here < radix * span)
        value = jnp.where(take, arrived, value)
        span *= radix
    return value


def butterfly_sum(value, axis, size):
    step = 1
    while step < size:
        pairs = [(i, i ^ step) for i in range(size)]
        value = value + lax.ppermute(value, axis, pairs)
        step *= 2
    return value


def halving_scatter(value, axis, size):
    here = lax.axis_index(axis)
    band = value.shape[0] // size
    blocks = value.reshape(size, band, value.shape[1])
    step = size // 2
    while step >= 1:
        halves = blocks.reshape(2, step, band, value.shape[1])
        high = ((here // step) % 2) == 1
        keep = jnp.where(high, halves[1], halves[0])
        send = jnp.where(high, halves[0], halves[1])
        pairs = [(i, i ^ step) for i in range(size)]
        blocks = keep + lax.ppermute(send, axis, pairs)
        step //= 2
    return blocks.reshape(band, value.shape[1])


def doubling_gather(value, axis, size):
    here = lax.axis_index(axis)
    step = 1
    while step < size:
        pairs = [(i, i ^ step) for i in range(size)]
        other = lax.ppermute(value, axis, pairs)
        high = ((here // step) % 2) == 1
        value = jnp.where(
            high,
            jnp.concatenate([other, value], 0),
            jnp.concatenate([value, other], 0),
        )
        step *= 2
    return value


def halved_lower(matrix):
    order = matrix.shape[0]
    keep = jnp.tril(jnp.ones((order, order), matrix.dtype)) - 0.5 * jnp.eye(
        order, dtype=matrix.dtype
    )
    return matrix * keep


def inverse_lower(block):
    ident = jnp.eye(block.shape[0], dtype=block.dtype)
    return lax.linalg.triangular_solve(block, ident, left_side=True, lower=True)


def block_adjoint(block, inverse, seed_adj):
    inner = halved_lower(jnp.dot(block.T, seed_adj, precision=exact_mode))
    middle = jnp.dot(inverse.T, inner, precision=exact_mode)
    return halved_lower(jnp.dot(middle, inverse, precision=exact_mode))


def make_per_device(n_row, n_col):
    def per_device(
        trail,
        row_one,
        row_two,
        diag_one,
        diag_two,
        adj_trail,
        adj_row_one,
        adj_row_two,
        adj_diag_one,
        adj_diag_two,
    ):
        panel = diag_one.shape[0]
        width = trail.shape[1]
        band = row_one.shape[0]
        last = width - panel
        col_here = lax.axis_index("col")
        row_start = lax.axis_index("row") * band
        root_one = n_col - 2
        root_two = n_col - 1
        here_one = col_here == root_one
        here_two = col_here == root_two
        full_one = doubling_gather(row_one, "row", n_row)
        full_two = doubling_gather(row_two, "row", n_row)

        def own_rows(matrix):
            return lax.dynamic_slice_in_dim(matrix, row_start, band, 0)

        def solve_panel(rows, inverse, root):
            local = jnp.dot(rows, inverse, precision=exact_mode).astype(jnp.bfloat16)
            head = local.shape[0] % (16 * n_col)
            tail = panel_broadcast(local[head:], n_col, root, n_col - 1 - root)
            if head == 0:
                return tail
            return jnp.concatenate([tree_broadcast(local[:head], "col", n_col, root), tail], 0)

        def summed_block(partial_value, root):
            rows_sum = butterfly_sum(partial_value, "row", n_row)
            return tree_broadcast(rows_sum, "col", n_col, root)

        inverse_two = inverse_lower(diag_two)
        solved_two = solve_panel(adj_trail[:, last:], inverse_two, root_two)
        partial_two = jnp.dot(solved_two.T, trail[:, last:], preferred_element_type=jnp.float32)
        rows_two = butterfly_sum(partial_two, "row", n_row)
        solved_late, rows_two = lax.optimization_barrier((solved_two, rows_two))
        seed_two = jnp.tril(adj_diag_two - tree_broadcast(rows_two, "col", n_col, root_two))
        grad_diag_two = block_adjoint(diag_two, inverse_two, seed_two)
        mirror_two = own_rows(grad_diag_two + grad_diag_two.T)
        rest_two = jnp.dot(mirror_two, full_two.astype(jnp.float32), precision=exact_mode)
        inverse_one = inverse_lower(diag_one)
        crossed = halving_scatter(
            jnp.dot(solved_late.T, trail, preferred_element_type=jnp.float32), "row", n_row
        )
        adj_two = adj_row_two - crossed - rest_two
        next_panel = adj_trail[:, last:] - jnp.dot(
            solved_two, full_two[:, last:], preferred_element_type=jnp.float32
        )
        stacked = jnp.concatenate([adj_two[:, last:], next_panel], 0)
        solved_one = solve_panel(stacked, inverse_one, root_one)
        head_rows = solved_one[:band]
        tail_rows = solved_one[band:]
        partial_one = jnp.dot(
            head_rows.T, row_two[:, last:], preferred_element_type=jnp.float32
        ) + jnp.dot(tail_rows.T, trail[:, last:], preferred_element_type=jnp.float32)
        rows_one = butterfly_sum(partial_one, "row", n_row)
        tail_late, rows_one = lax.optimization_barrier((tail_rows, rows_one))
        seed_one = jnp.tril(adj_diag_one - tree_broadcast(rows_one, "col", n_col, root_one))
        grad_diag_one = block_adjoint(diag_one, inverse_one, seed_one)
        mirror_one = own_rows(grad_diag_one + grad_diag_one.T)
        rest_one = jnp.dot(mirror_one, full_one.astype(jnp.float32), precision=exact_mode)
        head_update = jnp.dot(head_rows, full_one, preferred_element_type=jnp.float32)
        two_left = adj_two - head_update
        trail_left = adj_trail - jnp.dot(
            jnp.concatenate([solved_two, tail_late], 1),
            jnp.concatenate([full_two, full_one], 0),
            preferred_element_type=jnp.float32,
        )
        crossed_one = halving_scatter(
            jnp.dot(head_rows.T, row_two, preferred_element_type=jnp.float32)
            + jnp.dot(tail_rows.T, trail, preferred_element_type=jnp.float32),
            "row",
            n_row,
        )
        one_left = adj_row_one - crossed_one - rest_one
        trail_block = jnp.where(
            here_one,
            tail_rows.astype(jnp.float32),
            jnp.where(here_two, solved_two.astype(jnp.float32), trail_left[:, last:]),
        )
        grad_trail = jnp.concatenate([trail_left[:, :last], trail_block], 1).astype(jnp.bfloat16)
        zero_block = jnp.zeros((band, panel), jnp.float32)
        one_block = jnp.where(here_one | here_two, zero_block, one_left[:, last:])
        grad_row_one = jnp.concatenate([one_left[:, :last], one_block], 1)
        two_block = jnp.where(
            here_one, head_rows.astype(jnp.float32), jnp.where(here_two, zero_block, two_left[:, last:])
        )
        grad_row_two = jnp.concatenate([two_left[:, :last], two_block], 1)
        return (grad_trail, grad_row_one, grad_row_two, grad_diag_one, grad_diag_two)

    return per_device


def solution(mesh):
    in_specs = (
        P("row", "col"),
        P("row", "col"),
        P("row", "col"),
        P(),
        P(),
        P("row", "col"),
        P("row", "col"),
        P("row", "col"),
        P(),
        P(),
    )
    out_specs = (P("row", "col"), P("row", "col"), P("row", "col"), P(), P())
    return jax.shard_map(
        make_per_device(mesh.shape["row"], mesh.shape["col"]),
        mesh=mesh,
        in_specs=in_specs,
        out_specs=out_specs,
        check_vma=False,
    )
```

```python
import functools

import jax
import jax.numpy as jnp
from jax import lax
from jax.experimental import pallas as pl
from jax.experimental.pallas import tpu as pltpu
from jax.sharding import PartitionSpec as P

exact_mode = lax.Precision.HIGHEST


def spread_kernel(root, size, x_ref, y_ref, buf, recv_sem, send_sem):
    me = lax.axis_index("col")
    row = lax.axis_index("row")
    barrier = pltpu.get_barrier_semaphore()
    for step in range(1, size):
        pl.semaphore_signal(
            barrier,
            inc=1,
            device_id=(row, lax.rem(me + step, size)),
            device_id_type=pl.DeviceIdType.MESH,
        )
    pl.semaphore_wait(barrier, size - 1)
    rows = x_ref.shape[0] // size
    is_root = me == root

    def piece(p):
        return pl.ds(p * rows, rows)

    def copy(p, dest, src, phase):
        return pltpu.make_async_remote_copy(
            src_ref=src.at[piece(p)],
            dst_ref=buf.at[piece(p)],
            send_sem=send_sem.at[phase, dest],
            recv_sem=recv_sem.at[p],
            device_id=(row, dest),
            device_id_type=pl.DeviceIdType.MESH,
        )

    @pl.when(is_root)
    def _():
        for dest in range(size):
            if dest != root:
                copy(dest, dest, x_ref, 0).start()
        for dest in range(size):
            if dest != root:
                copy(root, dest, x_ref, 1).start()
        for dest in range(size):
            if dest != root:
                copy(dest, dest, x_ref, 0).wait_send()
                copy(root, dest, x_ref, 1).wait_send()
        y_ref[...] = x_ref[...]

    @pl.when(jnp.logical_not(is_root))
    def _():
        for own in range(size):
            if own == root:
                continue

            @pl.when(me == own)
            def _():
                copy(own, own, buf, 0).wait_recv()
                for dest in range(size):
                    if dest != root and dest != own:
                        copy(own, dest, buf, 1).start()
                for p in range(size):
                    if p != own:
                        copy(p, own, buf, 1).wait_recv()
                for dest in range(size):
                    if dest != root and dest != own:
                        copy(own, dest, buf, 1).wait_send()
        y_ref[...] = buf[...]


def panel_broadcast(value, size, root, call_id):
    return pl.pallas_call(
        functools.partial(spread_kernel, root, size),
        out_shape=jax.ShapeDtypeStruct(value.shape, value.dtype),
        in_specs=[pl.BlockSpec(memory_space=pltpu.VMEM)],
        out_specs=pl.BlockSpec(memory_space=pltpu.VMEM),
        scratch_shapes=[
            pltpu.VMEM(value.shape, value.dtype),
            pltpu.SemaphoreType.DMA((size,)),
            pltpu.SemaphoreType.DMA((2, size)),
        ],
        compiler_params=pltpu.CompilerParams(collective_id=call_id, has_side_effects=True),
    )(value)


def tree_broadcast(value, axis, size, root):
    here = lax.axis_index(axis) ^ root
    span = 1
    while span < size:
        radix = min(4, size // span)
        arrived = None
        for digit in range(1, radix):
            pairs = [(root ^ d, root ^ (d + digit * span)) for d in range(span)]
            part = lax.ppermute(value, axis, pairs)
            arrived = part if arrived is None else arrived + part
        take = (here >= span) & (here < radix * span)
        value = jnp.where(take, arrived, value)
        span *= radix
    return value


def butterfly_sum(value, axis, size):
    step = 1
    while step < size:
        pairs = [(i, i ^ step) for i in range(size)]
        value = value + lax.ppermute(value, axis, pairs)
        step *= 2
    return value


def halving_scatter(value, axis, size):
    here = lax.axis_index(axis)
    band = value.shape[0] // size
    blocks = value.reshape(size, band, value.shape[1])
    step = size // 2
    while step >= 1:
        halves = blocks.reshape(2, step, band, value.shape[1])
        high = ((here // step) % 2) == 1
        keep = jnp.where(high, halves[1], halves[0])
        send = jnp.where(high, halves[0], halves[1])
        pairs = [(i, i ^ step) for i in range(size)]
        blocks = keep + lax.ppermute(send, axis, pairs)
        step //= 2
    return blocks.reshape(band, value.shape[1])


def doubling_gather(value, axis, size):
    here = lax.axis_index(axis)
    step = 1
    while step < size:
        pairs = [(i, i ^ step) for i in range(size)]
        other = lax.ppermute(value, axis, pairs)
        high = ((here // step) % 2) == 1
        value = jnp.where(
            high,
            jnp.concatenate([other, value], 0),
            jnp.concatenate([value, other], 0),
        )
        step *= 2
    return value


def halved_lower(matrix):
    order = matrix.shape[0]
    keep = jnp.tril(jnp.ones((order, order), matrix.dtype)) - 0.5 * jnp.eye(
        order, dtype=matrix.dtype
    )
    return matrix * keep


def inverse_lower(block):
    ident = jnp.eye(block.shape[0], dtype=block.dtype)
    return lax.linalg.triangular_solve(block, ident, left_side=True, lower=True)


def block_adjoint(block, inverse, seed_adj):
    inner = halved_lower(jnp.dot(block.T, seed_adj, precision=exact_mode))
    middle = jnp.dot(inverse.T, inner, precision=exact_mode)
    return halved_lower(jnp.dot(middle, inverse, precision=exact_mode))


def make_per_device(n_row, n_col):
    def per_device(
        trail,
        row_one,
        row_two,
        diag_one,
        diag_two,
        adj_trail,
        adj_row_one,
        adj_row_two,
        adj_diag_one,
        adj_diag_two,
    ):
        panel = diag_one.shape[0]
        width = trail.shape[1]
        band = row_one.shape[0]
        last = width - panel
        col_here = lax.axis_index("col")
        row_start = lax.axis_index("row") * band
        root_one = n_col - 2
        root_two = n_col - 1
        here_one = col_here == root_one
        here_two = col_here == root_two
        full_one = doubling_gather(row_one, "row", n_row)
        full_two = doubling_gather(row_two, "row", n_row)

        def own_rows(matrix):
            return lax.dynamic_slice_in_dim(matrix, row_start, band, 0)

        def solve_panel(rows, inverse, root):
            local = jnp.dot(rows, inverse, precision=exact_mode).astype(jnp.bfloat16)
            head = local.shape[0] % (16 * n_col)
            tail = panel_broadcast(local[head:], n_col, root, n_col - 1 - root)
            if head == 0:
                return tail
            return jnp.concatenate([tree_broadcast(local[:head], "col", n_col, root), tail], 0)

        def summed_block(partial_value, root):
            rows_sum = butterfly_sum(partial_value, "row", n_row)
            return tree_broadcast(rows_sum, "col", n_col, root)

        inverse_two = inverse_lower(diag_two)
        solved_two = solve_panel(adj_trail[:, last:], inverse_two, root_two)
        partial_two = jnp.dot(solved_two.T, trail[:, last:], preferred_element_type=jnp.float32)
        rows_two = butterfly_sum(partial_two, "row", n_row)
        diag_one_late, rows_two = lax.optimization_barrier((diag_one, rows_two))
        inverse_one = inverse_lower(diag_one_late)
        seed_two = jnp.tril(adj_diag_two - tree_broadcast(rows_two, "col", n_col, root_two))
        grad_diag_two = block_adjoint(diag_two, inverse_two, seed_two)
        mirror_two = own_rows(grad_diag_two + grad_diag_two.T)
        rest_two = jnp.dot(mirror_two, full_two.astype(jnp.float32), precision=exact_mode)
        crossed = halving_scatter(
            jnp.dot(solved_two.T, trail, preferred_element_type=jnp.float32), "row", n_row
        )
        adj_two = adj_row_two - crossed - rest_two
        next_panel = adj_trail[:, last:] - jnp.dot(
            solved_two, full_two[:, last:], preferred_element_type=jnp.float32
        )
        stacked = jnp.concatenate([adj_two[:, last:], next_panel], 0)
        solved_one = solve_panel(stacked, inverse_one, root_one)
        head_rows = solved_one[:band]
        tail_rows = solved_one[band:]
        partial_one = jnp.dot(
            head_rows.T, row_two[:, last:], preferred_element_type=jnp.float32
        ) + jnp.dot(tail_rows.T, trail[:, last:], preferred_element_type=jnp.float32)
        rows_one = butterfly_sum(partial_one, "row", n_row)
        tail_late, rows_one = lax.optimization_barrier((tail_rows, rows_one))
        seed_one = jnp.tril(adj_diag_one - tree_broadcast(rows_one, "col", n_col, root_one))
        grad_diag_one = block_adjoint(diag_one, inverse_one, seed_one)
        mirror_one = own_rows(grad_diag_one + grad_diag_one.T)
        rest_one = jnp.dot(mirror_one, full_one.astype(jnp.float32), precision=exact_mode)
        head_update = jnp.dot(head_rows, full_one, preferred_element_type=jnp.float32)
        two_left = adj_two - head_update
        trail_left = adj_trail - jnp.dot(
            jnp.concatenate([solved_two, tail_late], 1),
            jnp.concatenate([full_two, full_one], 0),
            preferred_element_type=jnp.float32,
        )
        crossed_one = halving_scatter(
            jnp.dot(head_rows.T, row_two, preferred_element_type=jnp.float32)
            + jnp.dot(tail_rows.T, trail, preferred_element_type=jnp.float32),
            "row",
            n_row,
        )
        one_left = adj_row_one - crossed_one - rest_one
        trail_block = jnp.where(
            here_one,
            tail_rows.astype(jnp.float32),
            jnp.where(here_two, solved_two.astype(jnp.float32), trail_left[:, last:]),
        )
        grad_trail = jnp.concatenate([trail_left[:, :last], trail_block], 1).astype(jnp.bfloat16)
        zero_block = jnp.zeros((band, panel), jnp.float32)
        one_block = jnp.where(here_one | here_two, zero_block, one_left[:, last:])
        grad_row_one = jnp.concatenate([one_left[:, :last], one_block], 1)
        two_block = jnp.where(
            here_one, head_rows.astype(jnp.float32), jnp.where(here_two, zero_block, two_left[:, last:])
        )
        grad_row_two = jnp.concatenate([two_left[:, :last], two_block], 1)
        return (grad_trail, grad_row_one, grad_row_two, grad_diag_one, grad_diag_two)

    return per_device


def solution(mesh):
    in_specs = (
        P("row", "col"),
        P("row", "col"),
        P("row", "col"),
        P(),
        P(),
        P("row", "col"),
        P("row", "col"),
        P("row", "col"),
        P(),
        P(),
    )
    out_specs = (P("row", "col"), P("row", "col"), P("row", "col"), P(), P())
    return jax.shard_map(
        make_per_device(mesh.shape["row"], mesh.shape["col"]),
        mesh=mesh,
        in_specs=in_specs,
        out_specs=out_specs,
        check_vma=False,
    )
```

```python
import functools

import jax
import jax.numpy as jnp
from jax import lax
from jax.experimental import pallas as pl
from jax.experimental.pallas import tpu as pltpu
from jax.sharding import PartitionSpec as P

exact_mode = lax.Precision.HIGHEST


def spread_kernel(root, size, x_ref, y_ref, buf, recv_sem, send_sem):
    me = lax.axis_index("col")
    row = lax.axis_index("row")
    barrier = pltpu.get_barrier_semaphore()
    for step in range(1, size):
        pl.semaphore_signal(
            barrier,
            inc=1,
            device_id=(row, lax.rem(me + step, size)),
            device_id_type=pl.DeviceIdType.MESH,
        )
    pl.semaphore_wait(barrier, size - 1)
    rows = x_ref.shape[0] // size
    is_root = me == root

    def piece(p):
        return pl.ds(p * rows, rows)

    def copy(p, dest, src, phase):
        return pltpu.make_async_remote_copy(
            src_ref=src.at[piece(p)],
            dst_ref=buf.at[piece(p)],
            send_sem=send_sem.at[phase, dest],
            recv_sem=recv_sem.at[p],
            device_id=(row, dest),
            device_id_type=pl.DeviceIdType.MESH,
        )

    @pl.when(is_root)
    def _():
        for dest in range(size):
            if dest != root:
                copy(dest, dest, x_ref, 0).start()
        for dest in range(size):
            if dest != root:
                copy(root, dest, x_ref, 1).start()
        for dest in range(size):
            if dest != root:
                copy(dest, dest, x_ref, 0).wait_send()
                copy(root, dest, x_ref, 1).wait_send()
        y_ref[...] = x_ref[...]

    @pl.when(jnp.logical_not(is_root))
    def _():
        for own in range(size):
            if own == root:
                continue

            @pl.when(me == own)
            def _():
                copy(own, own, buf, 0).wait_recv()
                for dest in range(size):
                    if dest != root and dest != own:
                        copy(own, dest, buf, 1).start()
                for p in range(size):
                    if p != own:
                        copy(p, own, buf, 1).wait_recv()
                for dest in range(size):
                    if dest != root and dest != own:
                        copy(own, dest, buf, 1).wait_send()
        y_ref[...] = buf[...]


def panel_broadcast(value, size, root, call_id):
    return pl.pallas_call(
        functools.partial(spread_kernel, root, size),
        out_shape=jax.ShapeDtypeStruct(value.shape, value.dtype),
        in_specs=[pl.BlockSpec(memory_space=pltpu.VMEM)],
        out_specs=pl.BlockSpec(memory_space=pltpu.VMEM),
        scratch_shapes=[
            pltpu.VMEM(value.shape, value.dtype),
            pltpu.SemaphoreType.DMA((size,)),
            pltpu.SemaphoreType.DMA((2, size)),
        ],
        compiler_params=pltpu.CompilerParams(collective_id=call_id, has_side_effects=True),
    )(value)


def tree_broadcast(value, axis, size, root):
    here = lax.axis_index(axis) ^ root
    span = 1
    while span < size:
        radix = min(4, size // span)
        arrived = None
        for digit in range(1, radix):
            pairs = [(root ^ d, root ^ (d + digit * span)) for d in range(span)]
            part = lax.ppermute(value, axis, pairs)
            arrived = part if arrived is None else arrived + part
        take = (here >= span) & (here < radix * span)
        value = jnp.where(take, arrived, value)
        span *= radix
    return value


def butterfly_sum(value, axis, size):
    step = 1
    while step < size:
        pairs = [(i, i ^ step) for i in range(size)]
        value = value + lax.ppermute(value, axis, pairs)
        step *= 2
    return value


def halving_scatter(value, axis, size):
    here = lax.axis_index(axis)
    band = value.shape[0] // size
    blocks = value.reshape(size, band, value.shape[1])
    step = size // 2
    while step >= 1:
        halves = blocks.reshape(2, step, band, value.shape[1])
        high = ((here // step) % 2) == 1
        keep = jnp.where(high, halves[1], halves[0])
        send = jnp.where(high, halves[0], halves[1])
        pairs = [(i, i ^ step) for i in range(size)]
        blocks = keep + lax.ppermute(send.astype(jnp.bfloat16), axis, pairs).astype(jnp.float32)
        step //= 2
    return blocks.reshape(band, value.shape[1])


def doubling_gather(value, axis, size):
    here = lax.axis_index(axis)
    step = 1
    while step < size:
        pairs = [(i, i ^ step) for i in range(size)]
        other = lax.ppermute(value, axis, pairs)
        high = ((here // step) % 2) == 1
        value = jnp.where(
            high,
            jnp.concatenate([other, value], 0),
            jnp.concatenate([value, other], 0),
        )
        step *= 2
    return value


def halved_lower(matrix):
    order = matrix.shape[0]
    keep = jnp.tril(jnp.ones((order, order), matrix.dtype)) - 0.5 * jnp.eye(
        order, dtype=matrix.dtype
    )
    return matrix * keep


def inverse_lower(block):
    ident = jnp.eye(block.shape[0], dtype=block.dtype)
    return lax.linalg.triangular_solve(block, ident, left_side=True, lower=True)


def block_adjoint(block, inverse, seed_adj):
    inner = halved_lower(jnp.dot(block.T, seed_adj, precision=exact_mode))
    middle = jnp.dot(inverse.T, inner, precision=exact_mode)
    return halved_lower(jnp.dot(middle, inverse, precision=exact_mode))


def make_per_device(n_row, n_col):
    def per_device(
        trail,
        row_one,
        row_two,
        diag_one,
        diag_two,
        adj_trail,
        adj_row_one,
        adj_row_two,
        adj_diag_one,
        adj_diag_two,
    ):
        panel = diag_one.shape[0]
        width = trail.shape[1]
        band = row_one.shape[0]
        last = width - panel
        col_here = lax.axis_index("col")
        row_start = lax.axis_index("row") * band
        root_one = n_col - 2
        root_two = n_col - 1
        here_one = col_here == root_one
        here_two = col_here == root_two
        full_one = doubling_gather(row_one, "row", n_row)
        full_two = doubling_gather(row_two, "row", n_row)

        def own_rows(matrix):
            return lax.dynamic_slice_in_dim(matrix, row_start, band, 0)

        def solve_panel(rows, inverse, root):
            local = jnp.dot(rows, inverse, precision=exact_mode).astype(jnp.bfloat16)
            head = local.shape[0] % (16 * n_col)
            tail = panel_broadcast(local[head:], n_col, root, n_col - 1 - root)
            if head == 0:
                return tail
            return jnp.concatenate([tree_broadcast(local[:head], "col", n_col, root), tail], 0)

        def summed_block(partial_value, root):
            rows_sum = butterfly_sum(partial_value, "row", n_row)
            return tree_broadcast(rows_sum, "col", n_col, root)

        inverse_two = inverse_lower(diag_two)
        solved_two = solve_panel(adj_trail[:, last:], inverse_two, root_two)
        partial_two = jnp.dot(solved_two.T, trail[:, last:], preferred_element_type=jnp.float32)
        seed_two = jnp.tril(adj_diag_two - summed_block(partial_two, root_two))
        grad_diag_two = block_adjoint(diag_two, inverse_two, seed_two)
        mirror_two = own_rows(grad_diag_two + grad_diag_two.T)
        rest_two = jnp.dot(mirror_two, full_two.astype(jnp.float32), precision=exact_mode)
        inverse_one = inverse_lower(diag_one)
        crossed = halving_scatter(
            jnp.dot(solved_two.T, trail, preferred_element_type=jnp.float32), "row", n_row
        )
        adj_two = adj_row_two - crossed - rest_two
        next_panel = adj_trail[:, last:] - jnp.dot(
            solved_two, full_two[:, last:], preferred_element_type=jnp.float32
        )
        stacked = jnp.concatenate([adj_two[:, last:], next_panel], 0)
        solved_one = solve_panel(stacked, inverse_one, root_one)
        head_rows = solved_one[:band]
        tail_rows = solved_one[band:]
        partial_one = jnp.dot(
            head_rows.T, row_two[:, last:], preferred_element_type=jnp.float32
        ) + jnp.dot(tail_rows.T, trail[:, last:], preferred_element_type=jnp.float32)
        rows_one = butterfly_sum(partial_one, "row", n_row)
        tail_late, rows_one = lax.optimization_barrier((tail_rows, rows_one))
        seed_one = jnp.tril(adj_diag_one - tree_broadcast(rows_one, "col", n_col, root_one))
        grad_diag_one = block_adjoint(diag_one, inverse_one, seed_one)
        mirror_one = own_rows(grad_diag_one + grad_diag_one.T)
        rest_one = jnp.dot(mirror_one, full_one.astype(jnp.float32), precision=exact_mode)
        head_update = jnp.dot(head_rows, full_one, preferred_element_type=jnp.float32)
        two_left = adj_two - head_update
        trail_left = adj_trail - jnp.dot(
            jnp.concatenate([solved_two, tail_late], 1),
            jnp.concatenate([full_two, full_one], 0),
            preferred_element_type=jnp.float32,
        )
        crossed_one = halving_scatter(
            jnp.dot(head_rows.T, row_two, preferred_element_type=jnp.float32)
            + jnp.dot(tail_rows.T, trail, preferred_element_type=jnp.float32),
            "row",
            n_row,
        )
        one_left = adj_row_one - crossed_one - rest_one
        trail_block = jnp.where(
            here_one,
            tail_rows.astype(jnp.float32),
            jnp.where(here_two, solved_two.astype(jnp.float32), trail_left[:, last:]),
        )
        grad_trail = jnp.concatenate([trail_left[:, :last], trail_block], 1).astype(jnp.bfloat16)
        zero_block = jnp.zeros((band, panel), jnp.float32)
        one_block = jnp.where(here_one | here_two, zero_block, one_left[:, last:])
        grad_row_one = jnp.concatenate([one_left[:, :last], one_block], 1)
        two_block = jnp.where(
            here_one, head_rows.astype(jnp.float32), jnp.where(here_two, zero_block, two_left[:, last:])
        )
        grad_row_two = jnp.concatenate([two_left[:, :last], two_block], 1)
        return (grad_trail, grad_row_one, grad_row_two, grad_diag_one, grad_diag_two)

    return per_device


def solution(mesh):
    in_specs = (
        P("row", "col"),
        P("row", "col"),
        P("row", "col"),
        P(),
        P(),
        P("row", "col"),
        P("row", "col"),
        P("row", "col"),
        P(),
        P(),
    )
    out_specs = (P("row", "col"), P("row", "col"), P("row", "col"), P(), P())
    return jax.shard_map(
        make_per_device(mesh.shape["row"], mesh.shape["col"]),
        mesh=mesh,
        in_specs=in_specs,
        out_specs=out_specs,
        check_vma=False,
    )
```

```python
import functools

import jax
import jax.numpy as jnp
from jax import lax
from jax.experimental import pallas as pl
from jax.experimental.pallas import tpu as pltpu
from jax.sharding import PartitionSpec as P

exact_mode = lax.Precision.HIGHEST


def spread_kernel(root, size, x_ref, y_ref, buf, recv_sem, send_sem):
    me = lax.axis_index("col")
    row = lax.axis_index("row")
    barrier = pltpu.get_barrier_semaphore()
    for step in range(1, size):
        pl.semaphore_signal(
            barrier,
            inc=1,
            device_id=(row, lax.rem(me + step, size)),
            device_id_type=pl.DeviceIdType.MESH,
        )
    pl.semaphore_wait(barrier, size - 1)
    rows = x_ref.shape[0] // size
    is_root = me == root

    def piece(p):
        return pl.ds(p * rows, rows)

    def copy(p, dest, src, phase):
        return pltpu.make_async_remote_copy(
            src_ref=src.at[piece(p)],
            dst_ref=buf.at[piece(p)],
            send_sem=send_sem.at[phase, dest],
            recv_sem=recv_sem.at[p],
            device_id=(row, dest),
            device_id_type=pl.DeviceIdType.MESH,
        )

    @pl.when(is_root)
    def _():
        for dest in range(size):
            if dest != root:
                copy(dest, dest, x_ref, 0).start()
        for dest in range(size):
            if dest != root:
                copy(root, dest, x_ref, 1).start()
        for dest in range(size):
            if dest != root:
                copy(dest, dest, x_ref, 0).wait_send()
                copy(root, dest, x_ref, 1).wait_send()
        y_ref[...] = x_ref[...]

    @pl.when(jnp.logical_not(is_root))
    def _():
        for own in range(size):
            if own == root:
                continue

            @pl.when(me == own)
            def _():
                copy(own, own, buf, 0).wait_recv()
                for dest in range(size):
                    if dest != root and dest != own:
                        copy(own, dest, buf, 1).start()
                for p in range(size):
                    if p != own:
                        copy(p, own, buf, 1).wait_recv()
                for dest in range(size):
                    if dest != root and dest != own:
                        copy(own, dest, buf, 1).wait_send()
        y_ref[...] = buf[...]


def panel_broadcast(value, size, root, call_id):
    return pl.pallas_call(
        functools.partial(spread_kernel, root, size),
        out_shape=jax.ShapeDtypeStruct(value.shape, value.dtype),
        in_specs=[pl.BlockSpec(memory_space=pltpu.VMEM)],
        out_specs=pl.BlockSpec(memory_space=pltpu.VMEM),
        scratch_shapes=[
            pltpu.VMEM(value.shape, value.dtype),
            pltpu.SemaphoreType.DMA((size,)),
            pltpu.SemaphoreType.DMA((2, size)),
        ],
        compiler_params=pltpu.CompilerParams(collective_id=call_id, has_side_effects=True),
    )(value)


def tree_broadcast(value, axis, size, root):
    here = lax.axis_index(axis) ^ root
    span = 1
    while span < size:
        radix = min(4, size // span)
        arrived = None
        for digit in range(1, radix):
            pairs = [(root ^ d, root ^ (d + digit * span)) for d in range(span)]
            part = lax.ppermute(value, axis, pairs)
            arrived = part if arrived is None else arrived + part
        take = (here >= span) & (here < radix * span)
        value = jnp.where(take, arrived, value)
        span *= radix
    return value


def butterfly_sum(value, axis, size):
    step = 1
    while step < size:
        pairs = [(i, i ^ step) for i in range(size)]
        value = value + lax.ppermute(value, axis, pairs)
        step *= 2
    return value


def halving_scatter(value, axis, size):
    here = lax.axis_index(axis)
    band = value.shape[0] // size
    blocks = value.reshape(size, band, value.shape[1])
    step = size // 2
    while step >= 1:
        halves = blocks.reshape(2, step, band, value.shape[1])
        high = ((here // step) % 2) == 1
        keep = jnp.where(high, halves[1], halves[0])
        send = jnp.where(high, halves[0], halves[1])
        pairs = [(i, i ^ step) for i in range(size)]
        blocks = keep + lax.ppermute(send.astype(jnp.bfloat16), axis, pairs).astype(jnp.float32)
        step //= 2
    return blocks.reshape(band, value.shape[1])


def doubling_gather(value, axis, size):
    here = lax.axis_index(axis)
    step = 1
    while step < size:
        pairs = [(i, i ^ step) for i in range(size)]
        other = lax.ppermute(value, axis, pairs)
        high = ((here // step) % 2) == 1
        value = jnp.where(
            high,
            jnp.concatenate([other, value], 0),
            jnp.concatenate([value, other], 0),
        )
        step *= 2
    return value


def halved_lower(matrix):
    order = matrix.shape[0]
    keep = jnp.tril(jnp.ones((order, order), matrix.dtype)) - 0.5 * jnp.eye(
        order, dtype=matrix.dtype
    )
    return matrix * keep


def inverse_lower(block):
    ident = jnp.eye(block.shape[0], dtype=block.dtype)
    return lax.linalg.triangular_solve(block, ident, left_side=True, lower=True)


def block_adjoint(block, inverse, seed_adj):
    inner = halved_lower(jnp.dot(block.T, seed_adj, precision=exact_mode))
    middle = jnp.dot(inverse.T, inner, precision=exact_mode)
    return halved_lower(jnp.dot(middle, inverse, precision=exact_mode))


def make_per_device(n_row, n_col):
    def per_device(
        trail,
        row_one,
        row_two,
        diag_one,
        diag_two,
        adj_trail,
        adj_row_one,
        adj_row_two,
        adj_diag_one,
        adj_diag_two,
    ):
        panel = diag_one.shape[0]
        width = trail.shape[1]
        band = row_one.shape[0]
        last = width - panel
        col_here = lax.axis_index("col")
        row_start = lax.axis_index("row") * band
        root_one = n_col - 2
        root_two = n_col - 1
        here_one = col_here == root_one
        here_two = col_here == root_two
        full_one = doubling_gather(row_one, "row", n_row)
        full_two = doubling_gather(row_two, "row", n_row)

        def own_rows(matrix):
            return lax.dynamic_slice_in_dim(matrix, row_start, band, 0)

        def solve_panel(rows, inverse, root):
            local = jnp.dot(rows, inverse, precision=exact_mode).astype(jnp.bfloat16)
            head = local.shape[0] % (16 * n_col)
            tail = panel_broadcast(local[head:], n_col, root, n_col - 1 - root)
            if head == 0:
                return tail
            return jnp.concatenate([tree_broadcast(local[:head], "col", n_col, root), tail], 0)

        def summed_block(partial_value, root):
            rows_sum = butterfly_sum(partial_value, "row", n_row)
            sent = tree_broadcast(rows_sum.astype(jnp.bfloat16), "col", n_col, root)
            return sent.astype(jnp.float32)

        inverse_two = inverse_lower(diag_two)
        solved_two = solve_panel(adj_trail[:, last:], inverse_two, root_two)
        partial_two = jnp.dot(solved_two.T, trail[:, last:], preferred_element_type=jnp.float32)
        seed_two = jnp.tril(adj_diag_two - summed_block(partial_two, root_two))
        grad_diag_two = block_adjoint(diag_two, inverse_two, seed_two)
        mirror_two = own_rows(grad_diag_two + grad_diag_two.T)
        rest_two = jnp.dot(mirror_two, full_two.astype(jnp.float32), precision=exact_mode)
        inverse_one = inverse_lower(diag_one)
        crossed = halving_scatter(
            jnp.dot(solved_two.T, trail, preferred_element_type=jnp.float32), "row", n_row
        )
        adj_two = adj_row_two - crossed - rest_two
        next_panel = adj_trail[:, last:] - jnp.dot(
            solved_two, full_two[:, last:], preferred_element_type=jnp.float32
        )
        stacked = jnp.concatenate([adj_two[:, last:], next_panel], 0)
        solved_one = solve_panel(stacked, inverse_one, root_one)
        head_rows = solved_one[:band]
        tail_rows = solved_one[band:]
        partial_one = jnp.dot(
            head_rows.T, row_two[:, last:], preferred_element_type=jnp.float32
        ) + jnp.dot(tail_rows.T, trail[:, last:], preferred_element_type=jnp.float32)
        rows_one = butterfly_sum(partial_one, "row", n_row)
        tail_late, rows_one = lax.optimization_barrier((tail_rows, rows_one))
        sent_one = tree_broadcast(rows_one.astype(jnp.bfloat16), "col", n_col, root_one)
        seed_one = jnp.tril(adj_diag_one - sent_one.astype(jnp.float32))
        grad_diag_one = block_adjoint(diag_one, inverse_one, seed_one)
        mirror_one = own_rows(grad_diag_one + grad_diag_one.T)
        rest_one = jnp.dot(mirror_one, full_one.astype(jnp.float32), precision=exact_mode)
        head_update = jnp.dot(head_rows, full_one, preferred_element_type=jnp.float32)
        two_left = adj_two - head_update
        trail_left = adj_trail - jnp.dot(
            jnp.concatenate([solved_two, tail_late], 1),
            jnp.concatenate([full_two, full_one], 0),
            preferred_element_type=jnp.float32,
        )
        crossed_one = halving_scatter(
            jnp.dot(head_rows.T, row_two, preferred_element_type=jnp.float32)
            + jnp.dot(tail_rows.T, trail, preferred_element_type=jnp.float32),
            "row",
            n_row,
        )
        one_left = adj_row_one - crossed_one - rest_one
        trail_block = jnp.where(
            here_one,
            tail_rows.astype(jnp.float32),
            jnp.where(here_two, solved_two.astype(jnp.float32), trail_left[:, last:]),
        )
        grad_trail = jnp.concatenate([trail_left[:, :last], trail_block], 1).astype(jnp.bfloat16)
        zero_block = jnp.zeros((band, panel), jnp.float32)
        one_block = jnp.where(here_one | here_two, zero_block, one_left[:, last:])
        grad_row_one = jnp.concatenate([one_left[:, :last], one_block], 1)
        two_block = jnp.where(
            here_one, head_rows.astype(jnp.float32), jnp.where(here_two, zero_block, two_left[:, last:])
        )
        grad_row_two = jnp.concatenate([two_left[:, :last], two_block], 1)
        return (grad_trail, grad_row_one, grad_row_two, grad_diag_one, grad_diag_two)

    return per_device


def solution(mesh):
    in_specs = (
        P("row", "col"),
        P("row", "col"),
        P("row", "col"),
        P(),
        P(),
        P("row", "col"),
        P("row", "col"),
        P("row", "col"),
        P(),
        P(),
    )
    out_specs = (P("row", "col"), P("row", "col"), P("row", "col"), P(), P())
    return jax.shard_map(
        make_per_device(mesh.shape["row"], mesh.shape["col"]),
        mesh=mesh,
        in_specs=in_specs,
        out_specs=out_specs,
        check_vma=False,
    )
```
